512 devices in a mesh: dp: 128 (over y, z, core), mp: 4 (over x).
Axes of the slice: x: 4, y: 4, z: 16, core: 2. Of those that a mesh axis runs over, the one named last changes fastest.
Arguments:
- cams: int32 [768], replicated, may hold values from 5 to 11, as said below
- pack: int32 [6144], replicated, may hold values from 0 to 6143, as said below
- visible: int32 [768, 11, 4], P('dp'), may hold values from 0 to 1, as said below
- align: int32 [768, 4, 512], P('dp', None, 'mp'), may hold values from 0 to 511, as said below
- images: bfloat16 [6144, 32, 1024], P('dp', 'mp'), may hold values from -24 to 24
- cam_keys: bfloat16 [6144, 32, 256], P('dp', 'mp'), may hold values from -8 to 8
- neck_weight: bfloat16 [1024, 256], replicated, may hold values from -0.1875 to 0.1875
- bev_query: bfloat16 [512, 256], P('mp'), may hold values from -8 to 8
- prev_bev: bfloat16 [768, 512, 256], P('dp', 'mp'), may hold values from -6 to 6
- point_weight: bfloat16 [256, 32], replicated, may hold values from -0.375 to 0.375
- norm_gain: float32 [256], replicated, may hold values from 0.5 to 1.5
- out_grad: bfloat16 [768, 512, 256], P('dp', 'mp'), may hold values from -6 to 6
Outputs:
- bev_out: bfloat16 [768, 512, 256], P('dp', 'mp')
- neck_grad: float32 [1024, 256], P(('dp', 'mp'))
The draws below stay inside these ranges and needn't reach their ends.
Inputs may be any that keep to these rules, and one draw needn't show every extreme that they name: `cams`: the counts of all samples sum to 6144. `pack`: A permutation of the bin-slot positions; the bin of a position is position // 48. No bin holds more than 1 cameras of the samples of one owner (samples o * 6 to o * 6 + 5). `visible`: every grid row of a sample is seen by 1 to 3 of its cameras, some row by exactly 3; entries of camera slots j >= cams[s] are 0. `align`: cell numbers row * 128 + column of the sample's previous grid, in the same band of 1 row (row) as the query cell.
All inputs are finite; a program needn't handle non-finite values.
Results may differ from the reference program's by a relative error of at most 0.008.
Values may be sent and summed in bfloat16 or wider, within the bound.
No kernel may reach another device: no remote copies, remote signals or barrier semaphores. Data moves between devices by JAX's collectives and lax.ppermute only.
A program may use at most 64 MiB of HBM per device.

```python
import jax
import jax.numpy as jnp
from jax import lax

D = 1024
C = 256
HEADS = 8
KT = 4
MAXCAM = 11
SPD = 6
GW = 128
TPC = 32
RPD = 1
GRID = 512
GROWS = 4
SAMPLES = 768
BIN_CAMS = 48
CAMS = 6144
N_DP = 128


def sample_counts(key):
    base = jax.random.fold_in(key, 101)
    key_owner, key_order, key_delta = jax.random.split(base, 3)
    chosen = jax.random.randint(key_owner, (), 0, N_DP)
    sample_ids = jnp.arange(SAMPLES, dtype=jnp.int32)
    forced = sample_ids // SPD == chosen
    shuffled = jax.random.permutation(key_order, SAMPLES).astype(jnp.int32)
    shuffled = shuffled[jnp.argsort(forced[shuffled].astype(jnp.int32), stable=True)]
    camera_counts = jnp.where(forced, MAXCAM, 8).astype(jnp.int32)
    camera_counts = camera_counts.at[shuffled[:SPD]].set(MAXCAM - 6)
    remaining = shuffled[SPD:SAMPLES - SPD]
    deltas = jax.random.randint(key_delta, ((SAMPLES - 2 * SPD) // 2,), -3, 4)
    camera_counts = camera_counts.at[remaining[0::2]].set(8 + deltas)
    camera_counts = camera_counts.at[remaining[1::2]].set(8 - deltas)
    return camera_counts.astype(jnp.int32)


def draw_cams(key, part):
    return sample_counts(key)


def draw_pack(key, part):
    shuffle_bins = jax.random.permutation(jax.random.fold_in(key, 202), N_DP).astype(jnp.int32)
    turns = jax.random.randint(jax.random.fold_in(key, 203), (N_DP,), 0, BIN_CAMS)
    camera_ids = jnp.arange(CAMS, dtype=jnp.int32)
    bin_of = shuffle_bins[camera_ids % N_DP]
    slot_of = (camera_ids // N_DP + turns[bin_of]) % BIN_CAMS
    return (bin_of * BIN_CAMS + slot_of).astype(jnp.int32)


def draw_visible(key, part):
    camera_counts = sample_counts(key)[:, None]
    base = jax.random.fold_in(key, 303)
    key_shift, key_third, key_second, key_use, key_force = jax.random.split(base, 5)
    row_ids = jnp.arange(GROWS, dtype=jnp.int32)[None, :]
    shift = jax.random.randint(key_shift, (SAMPLES, 1), 0, GROWS)
    primary = (row_ids + shift) * camera_counts // GROWS % camera_counts
    secondary = (primary + 1) % camera_counts
    tertiary = jax.random.randint(key_third, (SAMPLES, GROWS), 0, camera_counts)
    use_second = jax.random.randint(key_second, (SAMPLES, GROWS), 0, 2) == 1
    use_third = jax.random.randint(key_use, (SAMPLES, GROWS), 0, 3) == 0
    force_row = jax.random.randint(key_force, (SAMPLES, 1), 0, GROWS)
    forced = row_ids == force_row
    tertiary = jnp.where(forced, (primary + 2) % camera_counts, tertiary)
    use_second = use_second | forced
    use_third = use_third | forced
    slot_ids = jnp.arange(MAXCAM, dtype=jnp.int32)[None, :, None]
    seen_mask = (slot_ids == primary[:, None, :]) | (slot_ids == secondary[:, None, :]) & use_second[:, None, :]
    seen_mask = seen_mask | (slot_ids == tertiary[:, None, :]) & use_third[:, None, :]
    return seen_mask.astype(jnp.int32)


def draw_align(key, part):
    base = jax.random.fold_in(key, 404)
    key_ego_row, key_ego_col, key_row, key_col = jax.random.split(base, 4)
    cells = jnp.arange(GRID, dtype=jnp.int32)[None, None, :]
    cell_rows = cells // GW
    cell_cols = cells % GW
    band_low = cell_rows // RPD * RPD
    ego_row = jax.random.randint(key_ego_row, (SAMPLES, 1, 1), -1, 2)
    ego_col = jax.random.randint(key_ego_col, (SAMPLES, 1, 1), -6, 7)
    jitter_row = jax.random.randint(key_row, (SAMPLES, KT, GRID), -1, 2)
    jitter_col = jax.random.randint(key_col, (SAMPLES, KT, GRID), -3, 4)
    target_row = jnp.clip(cell_rows + ego_row + jitter_row, band_low, band_low + RPD - 1)
    target_col = jnp.clip(cell_cols + ego_col + jitter_col, 0, GW - 1)
    aligned = target_row * GW + target_col
    aligned = aligned.at[:, 0, GRID - 1].set(GRID - 1)
    aligned = aligned.at[:, 0, 0].set(0)
    return aligned.astype(jnp.int32)


def draw_cam_keys(key, part):
    base = jax.random.fold_in(key, 505)
    values = jnp.clip(2.0 * jax.random.normal(base, (CAMS, TPC, C), jnp.float32), -8.0, 8.0)
    return values.astype(jnp.bfloat16)


def draw_bev_query(key, part):
    base = jax.random.fold_in(key, 707)
    key_values = jax.random.fold_in(base, 2)
    values = jnp.clip(jax.random.normal(key_values, (GRID, C), jnp.float32), -6.0, 6.0)
    return values.astype(jnp.bfloat16)


def with_spikes(drawn, key, source, target, parts, factor):
    owner, partner = [(jnp.arange(drawn.shape[position]) // (drawn.shape[position] // parts)).reshape([-1 if axis == position else 1 for axis in range(drawn.ndim)]) for position in (source, target)]
    chosen = jax.random.permutation(key, parts)[partner]
    strong = (owner == chosen) | (owner == (partner + parts // 2) % parts)
    return jnp.where(strong, factor * drawn, drawn)


def steps_of(key, extent, shards, smallest, largest):
    def one(position, shards_of):
        draws = jax.random.uniform(jax.random.fold_in(jax.random.fold_in(key, 6), position), (shards_of,), jnp.float32, smallest / len(shards), largest / len(shards))
        return jnp.repeat(jnp.exp(draws), extent[position] // shards_of).reshape((-1,) + (1,) * (len(extent) - position - 1))

    loudness = one(*shards[0])
    for cut in shards[1:]:
        loudness = loudness * one(*cut)
    return loudness


def gaussian(stream_key, extent, width, limit, cuts=(), held_as=jnp.bfloat16):
    entries = width * jax.random.normal(stream_key, extent, jnp.float32)
    if cuts:
        entries = entries * steps_of(stream_key, extent, cuts, -0.22, 0.18)
    return jnp.clip(entries, -limit, limit).astype(held_as)


def heavy_noise(rng, extent, scale, bound, pieces, heavy, kind=jnp.bfloat16):
    values = scale * jax.random.normal(rng, extent, jnp.float32)
    if pieces:
        values = values * steps_of(rng, extent, pieces, -0.22, 0.18)
    return jnp.clip(with_spikes(values, jax.random.fold_in(rng, 3), *heavy), -bound, bound).astype(kind)


def setup_inputs(seed: int = 0) -> dict:
    key_list = jax.random.split(jax.random.key(seed), 13)
    return {
        "cams": draw_cams(jax.random.fold_in(key_list[12], 71), 0),
        "pack": draw_pack(jax.random.fold_in(key_list[12], 71), 0),
        "visible": draw_visible(jax.random.fold_in(key_list[12], 71), 0),
        "align": draw_align(jax.random.fold_in(key_list[12], 71), 0),
        "images": heavy_noise(key_list[4], (CAMS, TPC, D), 1.0, 24.0, ((0, 128), (1, 4)), (0, 2, 128, 5.5)),
        "cam_keys": draw_cam_keys(jax.random.fold_in(key_list[12], 71), 0),
        "neck_weight": gaussian(key_list[6], (D, C), D ** -0.5, 0.1875),
        "bev_query": draw_bev_query(jax.random.fold_in(key_list[12], 71), 0),
        "prev_bev": gaussian(key_list[8], (SAMPLES, GRID, C), 1.0, 6.0, ((0, 128), (1, 4))),
        "point_weight": gaussian(key_list[9], (C, HEADS * KT), C ** -0.5, 0.375),
        "norm_gain": jnp.clip(1.0 + 0.1 * jax.random.normal(key_list[10], (C,), jnp.float32), 0.5, 1.5),
        "out_grad": gaussian(key_list[11], (SAMPLES, GRID, C), 1.0, 6.0, ((0, 128), (1, 4))),
    }


NORM_EPS = 1e-05
MASKED = -1e+30

def layer_norm(pre_norm, norm_gain):
    row_mean = lax.optimization_barrier(jnp.mean(pre_norm, axis=-1, keepdims=True))
    centred = pre_norm - row_mean
    spread = lax.optimization_barrier(jnp.mean(centred * centred, axis=-1, keepdims=True))
    return centred * lax.rsqrt(spread + NORM_EPS) * norm_gain

def reference(cams, pack, visible, align, images, cam_keys, neck_weight, bev_query, prev_bev, point_weight, norm_gain, out_grad):
    head_dim = C // HEADS
    scale_factor = float(head_dim) ** (-0.5)
    features = jnp.dot(images.reshape(CAMS * TPC, D), neck_weight, preferred_element_type=jnp.float32)
    features = features.astype(jnp.bfloat16).reshape(CAMS, TPC, C)
    starts = (jnp.cumsum(cams) - cams).astype(jnp.int32)
    modulation = jax.nn.sigmoid(jnp.dot(bev_query, point_weight, preferred_element_type=jnp.float32)).reshape(GRID, HEADS, KT)
    grid_rows = (jnp.arange(GRID, dtype=jnp.int32) // GW).astype(jnp.int32)
    query_heads = bev_query.astype(jnp.float32).reshape(GRID, HEADS, head_dim)
    query_base = bev_query.astype(jnp.float32)
    camera_slot = jnp.arange(MAXCAM, dtype=jnp.int32)

    def one_sample(inputs):
        cam_count, start_cam, seen_by, aligned, previous, cotangent = inputs
        is_live = camera_slot < cam_count
        camera_ids = jnp.where(is_live, start_cam + camera_slot, 0).astype(jnp.int32)
        positions = pack[camera_ids].astype(jnp.int32)
        key_heads = cam_keys[positions].astype(jnp.float32).reshape(MAXCAM * TPC, HEADS, head_dim)
        value_heads = features[positions].astype(jnp.float32).reshape(MAXCAM * TPC, HEADS, head_dim)
        seen_mask = (seen_by[:, grid_rows] > 0) & is_live[:, None]
        seen_mask = jnp.repeat(seen_mask, TPC, axis=0).T
        scores = jnp.einsum('qhd,khd->hqk', query_heads, key_heads) * scale_factor
        scores = jnp.where(seen_mask[None], scores, MASKED)
        row_max = lax.optimization_barrier(jnp.max(scores, axis=-1, keepdims=True))
        raised = jnp.exp(scores - row_max)
        attn_probs = (raised / lax.optimization_barrier(jnp.sum(raised, axis=-1, keepdims=True))).astype(jnp.bfloat16)
        probs_wide = lax.optimization_barrier(attn_probs).astype(jnp.float32)
        cross_out = jnp.einsum('hqk,khd->qhd', probs_wide, value_heads).reshape(GRID, C)
        picked = previous[aligned].astype(jnp.float32).reshape(KT, GRID, HEADS, head_dim)
        temporal = jnp.einsum('qhk,kqhd->qhd', modulation, picked).reshape(GRID, C)
        pre_norm = query_base + cross_out + temporal
        normed, pull_back = jax.vjp(lambda pre_value: layer_norm(pre_value, norm_gain), pre_norm)
        pre_grad, = pull_back(cotangent.astype(jnp.float32))
        cross_grad = lax.optimization_barrier(pre_grad.astype(jnp.bfloat16)).astype(jnp.float32)
        cross_grad = cross_grad.reshape(GRID, HEADS, head_dim)
        value_grad = jnp.einsum('hqk,qhd->khd', probs_wide, cross_grad).reshape(MAXCAM, TPC, C).astype(jnp.bfloat16)
        targets = jnp.where(is_live, positions, CAMS).astype(jnp.int32)
        return (normed.astype(jnp.bfloat16), value_grad, targets)
    bev_out, value_grads, targets = lax.map(one_sample, (cams, starts, visible, align, prev_bev, out_grad))
    feature_grad = jnp.zeros((CAMS + 1, TPC, C), jnp.bfloat16)
    feature_grad = feature_grad.at[targets.reshape(SAMPLES * MAXCAM)].set(value_grads.reshape(SAMPLES * MAXCAM, TPC, C))
    flat_grad = feature_grad[:CAMS].reshape(CAMS * TPC, C)
    neck_grad = jnp.dot(images.reshape(CAMS * TPC, D).T, flat_grad, preferred_element_type=jnp.float32) / SAMPLES
    return (bev_out, neck_grad)
```

```python
import jax
import jax.numpy as jnp
from jax import lax
from jax.experimental import pallas as pl
from jax.experimental.pallas import tpu as pltpu
from jax.sharding import PartitionSpec as P

HEADS = 8
KT = 4
SEEN = 3

NORM_EPS = 1e-05
MASKED = -1e30
BF16 = jnp.bfloat16
F32 = jnp.float32
I32 = jnp.int32


def dot(a, b, a_dim=1, b_dim=0):
    return lax.dot_general(a, b, (((a_dim,), (b_dim,)), ((), ())), preferred_element_type=F32)


def iota(shape, dim):
    return lax.broadcasted_iota(I32, shape, dim)


def vmem():
    return pl.BlockSpec(memory_space=pltpu.VMEM)


def smem():
    return pl.BlockSpec(memory_space=pltpu.SMEM)


def call(body, outs, *args, specs=None, scratch=(), cost=(1 << 20, 1 << 20)):
    return pl.pallas_call(
        body,
        out_shape=outs,
        in_specs=specs or [vmem()] * len(args),
        out_specs=jax.tree.map(lambda _: vmem(), outs),
        scratch_shapes=scratch,
        cost_estimate=pl.CostEstimate(flops=cost[0], bytes_accessed=cost[1], transcendentals=0),
    )(*args)


def pack_kernel(bin_ref, cams_ref, pack_ref, image_ref, key_ref, weight_ref, lane_ref, target_ref):
    samples, cameras = cams_ref.shape[1], pack_ref.shape[1]
    rows, channels = key_ref.shape
    lanes = lane_ref.shape[0]
    owners = lanes // target_ref.shape[0]
    quarter = target_ref.shape[0]
    slots = rows // quarter
    spd = samples // owners
    counts = cams_ref[...].astype(F32)
    before = iota((owners, samples), 1) < iota((owners, samples), 0) * spd
    start = jnp.sum(jnp.where(before, counts, 0.0), axis=1, keepdims=True)
    begun = start <= iota((owners, cameras), 1).astype(F32)
    owner = jnp.sum(begun.astype(F32), axis=0, keepdims=True) - 1.0
    here = (pack_ref[...] - bin_ref[0] * slots) == iota((slots, cameras), 0)
    owner_of = dot(jnp.broadcast_to(owner, (8, cameras)).astype(BF16), here.astype(F32).astype(BF16), 1, 1)
    spread = (iota((slots, rows), 1) // quarter == iota((slots, rows), 0)).astype(F32).astype(BF16)
    owner_of = dot(owner_of.astype(BF16), spread).astype(I32)
    target = owner_of * quarter + iota((8, rows), 1) % quarter
    target_ref[...] = target
    place = (iota((lanes, rows), 0) == target[:1]).astype(F32).astype(BF16)
    features = dot(image_ref[...], weight_ref[...]).astype(BF16)
    lane_ref[:, :channels] = dot(place, features).astype(BF16)
    lane_ref[:, channels:] = dot(place, key_ref[...]).astype(BF16)


def temporal_kernel(band_ref, query_ref, point_ref, prev_ref, align_ref, base_ref):
    samples, cells, channels = prev_ref.shape
    query = query_ref[...]
    head_dim = channels // HEADS
    wide = query.astype(F32)
    gates = []
    for k in range(KT):
        shape = (HEADS * KT, channels)
        pick = iota(shape, 0) == (iota(shape, 1) // head_dim) * KT + k
        weight = dot(point_ref[...], pick.astype(F32).astype(BF16)).astype(BF16)
        gates.append(jax.nn.sigmoid(dot(query, weight)))
    for m in range(samples):
        total = wide
        for k in range(KT):
            cell = align_ref[m, k : k + 1, :] - band_ref[0] * cells
            pick = (iota((cells, cells), 0) == cell).astype(F32).astype(BF16)
            total = total + gates[k] * dot(pick, prev_ref[m], 0, 0)
        base_ref[m] = total


def select_kernel(target_ref, lane_ref, out_ref):
    pick = (iota((out_ref.shape[0], lane_ref.shape[0]), 1) == target_ref[...]).astype(F32).astype(BF16)
    out_ref[...] = dot(pick, lane_ref[...]).astype(BF16)


def attention_kernel(count_ref, kv_ref, base_ref, cotangent_ref, query_ref, gain_ref, out_ref, grad_ref):
    parts, rows, width = kv_ref.shape
    channels = width // 2
    keys = parts * rows
    head_dim = channels // HEADS
    quarter = rows // SEEN
    count = count_ref[pl.program_id(0)]
    query, gain = query_ref[...], gain_ref[...]
    queries = query.shape[0]
    lane_head = iota((1, channels), 1) // head_dim
    masks = [(lane_head == h).astype(F32) for h in range(HEADS)]
    values = kv_ref[:, :, :channels].reshape(keys, channels)
    ray = kv_ref[:, :, channels:].reshape(keys, channels)
    ray = jnp.concatenate([ray * mask.astype(BF16) for mask in masks], axis=0)
    values = jnp.concatenate([values * mask.astype(BF16) for mask in masks], axis=0)
    scores = dot(ray, query, 1, 1) * (float(head_dim) ** -0.5)
    kept = iota((keys, queries), 0) % rows // quarter < count
    scores = jnp.where(kept[None], scores.reshape(HEADS, keys, queries), MASKED)
    raised = jnp.exp(scores - jnp.max(scores, axis=1, keepdims=True))
    probs = (raised / jnp.sum(raised, axis=1, keepdims=True)).astype(BF16)
    probs = probs.reshape(HEADS * keys, queries)
    pre_norm = base_ref[0] + dot(probs, values, 0, 0)
    centred = pre_norm - jnp.mean(pre_norm, axis=1, keepdims=True)
    scale = lax.rsqrt(jnp.mean(centred * centred, axis=1, keepdims=True) + NORM_EPS)
    unit = centred * scale
    out_ref[0] = (unit * gain).astype(BF16)
    pull = cotangent_ref[0].astype(F32) * gain
    pull = pull - jnp.mean(pull, axis=1, keepdims=True) - unit * jnp.mean(pull * unit, axis=1, keepdims=True)
    spread = dot(probs, (pull * scale).astype(BF16))
    total = spread[:keys] * masks[0]
    for h in range(1, HEADS):
        total = total + spread[h * keys : (h + 1) * keys] * masks[h]
    grad_ref[...] = total.astype(BF16).reshape(parts, rows, channels)


def return_kernel(target_ref, grad_ref, lane_ref):
    pick = (iota((lane_ref.shape[0], grad_ref.shape[0]), 0) == target_ref[...]).astype(F32).astype(BF16)
    lane_ref[...] = dot(pick, grad_ref[...]).astype(BF16)


def neck_kernel(target_ref, lane_ref, image_ref, out_ref, sum_ref):
    pick = (iota((lane_ref.shape[0], image_ref.shape[0]), 0) == target_ref[:1]).astype(F32).astype(BF16)
    grads = dot(pick, lane_ref[...], 0, 0).astype(BF16)
    total = dot(image_ref[...], grads, 0, 0)
    cores, pieces, chips, _ = out_ref.shape
    half = sum_ref.shape[2]
    for i in range(sum_ref.shape[0]):
        sum_ref[i] = total[:, i * half : (i + 1) * half]
        for c in range(cores):
            for j in range(pieces):
                out_ref[c, j, :, i * half : (i + 1) * half] = sum_ref.at[i][
                    pl.ds(c * pieces + j, chips, stride=cores * pieces), :
                ]


def on_device(
    cams,
    pack,
    visible,
    align,
    images,
    cam_keys,
    neck_weight,
    bev_query,
    prev_bev,
    point_weight,
    norm_gain,
    out_grad,
):
    owners = lax.axis_size("dp")
    bands = lax.axis_size("mp")
    owner_id = lax.axis_index("dp").astype(I32)
    band_id = lax.axis_index("mp").astype(I32)
    samples, max_cams, _ = visible.shape
    slots, quarter, depth = images.shape
    channels = neck_weight.shape[1]
    queries = bev_query.shape[0]
    rows = slots * quarter
    flat_images = images.reshape(rows, depth)
    lanes, target = call(
        pack_kernel,
        (
            jax.ShapeDtypeStruct((owners * quarter, 2 * channels), BF16),
            jax.ShapeDtypeStruct((8, rows), I32),
        ),
        owner_id[None],
        cams[None],
        pack[None],
        flat_images,
        cam_keys.reshape(rows, channels),
        neck_weight,
        specs=[smem()] + [vmem()] * 5,
    )
    got = lax.all_to_all(
        lanes.reshape(owners, quarter, 2 * channels), "dp", split_axis=0, concat_axis=0, tiled=True
    )
    base = call(
        temporal_kernel,
        jax.ShapeDtypeStruct((samples, queries, channels), F32),
        band_id[None],
        bev_query,
        point_weight,
        prev_bev,
        align,
        specs=[smem()] + [vmem()] * 4,
        cost=(1 << 30, 1 << 22),
    )
    first = owner_id * samples
    sample_ids = jnp.arange(cams.shape[0], dtype=I32)
    start = jnp.sum(jnp.where(sample_ids < first, cams, 0))
    local = lax.dynamic_slice(cams, (first,), (samples,))
    window = samples * max_cams
    padded = jnp.concatenate([pack, jnp.zeros((window,), I32)])
    bins = lax.dynamic_slice(padded, (start,), (window,)) // slots
    member = jnp.arange(samples, dtype=I32)
    offset = jnp.sum(jnp.where(member[None, :] < member[:, None], local[None, :], 0), axis=1)
    camera = jnp.arange(max_cams, dtype=I32)
    seen = (visible > 0).astype(I32)
    earlier = (camera[:, None] < camera[None, :]).astype(I32)
    rank = jnp.sum(seen[:, :, None, :] * earlier[None, :, :, None], axis=1)
    place = jnp.arange(SEEN, dtype=I32)
    chosen = (rank[:, :, :, None] == place) & (seen[:, :, :, None] > 0)
    position = jnp.sum(
        jnp.where(chosen, offset[:, None, None, None] + camera[None, :, None, None] + 1, 0), axis=1
    )
    in_window = position[..., None] == jnp.arange(1, window + 1, dtype=I32)
    lane_of = jnp.sum(jnp.where(in_window, bins + 1, 0), axis=-1) - 1
    lane_of = lane_of.transpose(1, 0, 2).reshape(bands * samples * SEEN)
    count = lax.dynamic_slice_in_dim(jnp.sum(seen, axis=1), band_id, 1, axis=1)[:, 0]
    token = jnp.arange(quarter, dtype=I32)
    picks = jnp.where(lane_of[:, None] >= 0, lane_of[:, None] * quarter + token, -1).reshape(-1)
    piece = samples * SEEN * quarter
    chosen_kv = call(
        select_kernel,
        jax.ShapeDtypeStruct((bands * piece, 2 * channels), BF16),
        picks[:, None],
        got.reshape(owners * quarter, 2 * channels),
    )
    kv = lax.all_to_all(
        chosen_kv.reshape(bands, piece, 2 * channels), "mp", split_axis=0, concat_axis=0, tiled=True
    )
    step = SEEN * quarter
    bev_out, grads = pl.pallas_call(
        attention_kernel,
        grid_spec=pltpu.PrefetchScalarGridSpec(
            num_scalar_prefetch=1,
            grid=(samples,),
            in_specs=[
                pl.BlockSpec((bands, step, 2 * channels), lambda m, _: (0, m, 0)),
                pl.BlockSpec((1, queries, channels), lambda m, _: (m, 0, 0)),
                pl.BlockSpec((1, queries, channels), lambda m, _: (m, 0, 0)),
                pl.BlockSpec((queries, channels), lambda m, _: (0, 0)),
                pl.BlockSpec((1, channels), lambda m, _: (0, 0)),
            ],
            out_specs=[
                pl.BlockSpec((1, queries, channels), lambda m, _: (m, 0, 0)),
                pl.BlockSpec((bands, step, channels), lambda m, _: (0, m, 0)),
            ],
        ),
        out_shape=(
            jax.ShapeDtypeStruct((samples, queries, channels), BF16),
            jax.ShapeDtypeStruct((bands, piece, channels), BF16),
        ),
    )(count, kv, base, out_grad, bev_query, norm_gain[None])
    grads = lax.all_to_all(grads, "mp", split_axis=0, concat_axis=0, tiled=True)
    back = call(
        return_kernel,
        jax.ShapeDtypeStruct((owners * quarter, channels), BF16),
        picks[None],
        grads.reshape(bands * piece, channels),
    )
    back = lax.all_to_all(
        back.reshape(owners, quarter, channels), "dp", split_axis=0, concat_axis=0, tiled=True
    )
    chips = owners // 2
    share = depth // (owners * bands)
    neck = call(
        neck_kernel,
        jax.ShapeDtypeStruct((2, bands * share, chips, channels), F32),
        target,
        back.reshape(owners * quarter, channels),
        flat_images,
        scratch=[pltpu.VMEM((channels // 128, depth, 128), F32)],
    )
    pairs = [[2 * i, 2 * i + 1] for i in range(chips)]
    neck = lax.all_to_all(
        neck.reshape(2, bands * share * chips, channels),
        "dp",
        split_axis=0,
        concat_axis=0,
        tiled=True,
        axis_index_groups=pairs,
    )
    neck = jnp.sum(neck, axis=0).reshape(bands, share * chips, channels)
    neck = lax.all_to_all(neck, "mp", split_axis=0, concat_axis=0, tiled=True)
    neck = jnp.sum(neck, axis=0).reshape(share, chips, channels).transpose(1, 0, 2)
    sides = [[2 * i + c for i in range(chips)] for c in range(2)]
    neck = lax.all_to_all(
        neck, "dp", split_axis=0, concat_axis=0, tiled=True, axis_index_groups=sides
    )
    return bev_out, jnp.sum(neck, axis=0) / cams.shape[0]


def solution(mesh):
    return jax.shard_map(
        on_device,
        mesh=mesh,
        in_specs=(
            P(),
            P(),
            P("dp", None, None),
            P("dp", None, "mp"),
            P("dp", "mp", None),
            P("dp", "mp", None),
            P(),
            P("mp", None),
            P("dp", "mp", None),
            P(),
            P(),
            P("dp", "mp", None),
        ),
        out_specs=(P("dp", "mp", None), P(("dp", "mp"), None)),
        check_vma=False,
    )
```

```python
import functools

import jax
import jax.numpy as jnp
from jax import lax
from jax.experimental import pallas as pl
from jax.experimental.pallas import tpu as pltpu
from jax.sharding import PartitionSpec as P

HEADS = 8
KT = 4
CORES = 2
Y_CHIPS = 4
SEEN = 3

NORM_EPS = 1e-05
MASKED = -1e30
BF16 = jnp.bfloat16
F32 = jnp.float32
I32 = jnp.int32


def dot(a, b, a_dim=1, b_dim=0):
    return lax.dot_general(a, b, (((a_dim,), (b_dim,)), ((), ())), preferred_element_type=F32)


def iota(shape, dim):
    return lax.broadcasted_iota(I32, shape, dim)


def vmem():
    return pl.BlockSpec(memory_space=pltpu.VMEM)


def smem():
    return pl.BlockSpec(memory_space=pltpu.SMEM)


def on_chip(shape, dtype):
    return pltpu.VMEM(shape, dtype)


def call(body, outs, *args, specs=None, scratch=(), cost=(1 << 20, 1 << 20), pinned=True):
    specs = specs or [vmem()] * len(args)
    if pinned:
        args = [
            pltpu.with_memory_space_constraint(arg, spec.memory_space) for arg, spec in zip(args, specs)
        ]
    return pl.pallas_call(
        body,
        out_shape=outs,
        in_specs=specs,
        out_specs=jax.tree.map(lambda _: vmem(), outs),
        scratch_shapes=scratch,
        cost_estimate=pl.CostEstimate(flops=cost[0], bytes_accessed=cost[1], transcendentals=0),
    )(*args)


def pack_kernel(
    bin_ref,
    cams_ref,
    pack_ref,
    image_hbm,
    key_hbm,
    weight_hbm,
    lane_ref,
    owner_ref,
    image_ref,
    key_ref,
    weight_ref,
    sems,
):
    moves = [
        pltpu.make_async_copy(source, target, sems.at[i])
        for i, (source, target) in enumerate(
            ((image_hbm, image_ref), (weight_hbm, weight_ref), (key_hbm, key_ref))
        )
    ]
    for move in moves:
        move.start()
    cameras = pack_ref.shape[1]
    rows, channels = key_ref.shape
    slots = owner_ref.shape[1]
    quarter = rows // slots
    lanes = lane_ref.shape[0]
    owners = lanes // quarter
    groups, width = cams_ref.shape
    spd = groups * width // owners
    first = iota((owners, width), 0) * spd
    before = jnp.zeros((owners, width), F32)
    for g in range(groups):
        counts = cams_ref[g : g + 1, :].astype(F32)
        before += jnp.where(iota((owners, width), 1) + g * width < first, counts, 0.0)
    start = jnp.sum(before, axis=1, keepdims=True)
    here = (pack_ref[...] - bin_ref[0] * slots) == iota((slots, cameras), 0)
    here = here.astype(F32).astype(BF16)
    number = iota((8, cameras), 1)
    high = dot((number // 64).astype(F32).astype(BF16), here, 1, 1)
    low = dot((number % 64).astype(F32).astype(BF16), here, 1, 1)
    camera = (high * 64.0 + low)[:1]
    owner = jnp.sum((start <= camera).astype(F32), axis=0, keepdims=True) - 1.0
    owner = jnp.broadcast_to(owner, (8, slots))
    owner_ref[...] = owner.astype(I32)
    spread = (iota((slots, rows), 1) // quarter == iota((slots, rows), 0)).astype(F32).astype(BF16)
    target = dot(owner.astype(BF16), spread).astype(I32) * quarter + iota((8, rows), 1) % quarter
    place = (iota((lanes, rows), 0) == target[:1]).astype(F32).astype(BF16)
    moves[0].wait()
    moves[1].wait()
    features = dot(image_ref[...], weight_ref[...]).astype(BF16)
    lane_ref[:, :channels] = dot(place, features).astype(BF16)
    moves[2].wait()
    lane_ref[:, channels:] = dot(place, key_ref[...]).astype(BF16)


def turn_kernel(image_ref, out_ref, turned_ref, *, chips, depth, bands, share):
    turned = image_ref[...].astype(F32).T
    width = turned_ref.shape[2]
    for g in range(turned_ref.shape[0]):
        turned_ref[g] = turned[:, g * width : (g + 1) * width]
    step = CORES * bands * share
    at = 0
    for c in range(CORES):
        for y in range(chips):
            for j in range(bands * share):
                first = y * depth * step + c * bands * share + j
                for g in range(turned_ref.shape[0]):
                    part = turned_ref.at[g][pl.ds(first, depth, stride=step), :]
                    out_ref[at : at + depth, g * width : (g + 1) * width] = part.astype(BF16)
                at += depth


def temporal_kernel(band_ref, query_ref, point_ref, prev_ref, align_ref, base_ref):
    samples, cells, channels = prev_ref.shape
    query = query_ref[...]
    head_dim = channels // HEADS
    wide = query.astype(F32)
    gates = []
    for k in range(KT):
        shape = (HEADS * KT, channels)
        pick = iota(shape, 0) == (iota(shape, 1) // head_dim) * KT + k
        weight = dot(point_ref[...], pick.astype(F32).astype(BF16)).astype(BF16)
        gates.append(jax.nn.sigmoid(dot(query, weight)))
    for m in range(samples):
        total = wide
        for k in range(KT):
            cell = align_ref[m, k : k + 1, :] - band_ref[0] * cells
            pick = (iota((cells, cells), 0) == cell).astype(F32).astype(BF16)
            total = total + gates[k] * dot(pick, prev_ref[m], 0, 0)
        base_ref[m] = total


def select_kernel(source_ref, lane_ref, out_ref):
    for e in range(out_ref.shape[0]):
        out_ref[e] = lane_ref[source_ref[e]]


def attention_kernel(
    count_ref, kv_ref, base_ref, cotangent_ref, query_ref, gain_ref, out_ref, grad_ref
):
    parts, rows, width = kv_ref.shape
    samples, queries, channels = base_ref.shape
    step = rows // samples
    keys = parts * step
    head_dim = channels // HEADS
    quarter = step // SEEN
    query, gain = query_ref[...], gain_ref[...]
    lane_head = iota((1, channels), 1) // head_dim
    masks = [(lane_head == h).astype(F32) for h in range(HEADS)]
    place = iota((keys, queries), 0) % step // quarter
    for m in range(samples):
        here = slice(m * step, (m + 1) * step)
        values = kv_ref[:, here, :channels].reshape(keys, channels)
        ray = kv_ref[:, here, channels:].reshape(keys, channels)
        ray = jnp.concatenate([ray * mask.astype(BF16) for mask in masks], axis=0)
        values = jnp.concatenate([values * mask.astype(BF16) for mask in masks], axis=0)
        scores = dot(ray, query, 1, 1) * (float(head_dim) ** -0.5)
        scores = jnp.where((place < count_ref[m])[None], scores.reshape(HEADS, keys, queries), MASKED)
        raised = jnp.exp(scores - jnp.max(scores, axis=1, keepdims=True))
        probs = (raised * (1.0 / jnp.sum(raised, axis=1, keepdims=True))).astype(BF16)
        probs = probs.reshape(HEADS * keys, queries)
        pre_norm = base_ref[m] + dot(probs, values, 0, 0)
        centred = pre_norm - jnp.mean(pre_norm, axis=1, keepdims=True)
        scale = lax.rsqrt(jnp.mean(centred * centred, axis=1, keepdims=True) + NORM_EPS)
        unit = centred * scale
        out_ref[m] = (unit * gain).astype(BF16)
        pull = cotangent_ref[m].astype(F32) * gain
        pull = (
            pull
            - jnp.mean(pull, axis=1, keepdims=True)
            - unit * jnp.mean(pull * unit, axis=1, keepdims=True)
        )
        spread = dot(probs, (pull * scale).astype(BF16))
        total = spread[:keys] * masks[0]
        for h in range(1, HEADS):
            total = total + spread[h * keys : (h + 1) * keys] * masks[h]
        grad_ref[:, here, :] = total.astype(BF16).reshape(parts, step, channels)


def return_kernel(source_ref, grad_ref, lane_ref, sum_ref):
    sum_ref[...] = jnp.zeros(sum_ref.shape, F32)
    for e in range(grad_ref.shape[0]):
        lane = source_ref[e]
        sum_ref[lane] = sum_ref[lane] + grad_ref[e].astype(F32)
    lane_ref[...] = sum_ref[...].astype(BF16)


def neck_kernel(owner_ref, lane_ref, turned_ref, out_ref, grad_ref):
    quarter = lane_ref.shape[1]
    for s in range(grad_ref.shape[0] // quarter):
        grad_ref[s * quarter : (s + 1) * quarter, :] = lane_ref[owner_ref[s]]
    out_ref[...] = dot(turned_ref[...], grad_ref[...])


def on_device(
    cams,
    pack,
    visible,
    align,
    images,
    cam_keys,
    neck_weight,
    bev_query,
    prev_bev,
    point_weight,
    norm_gain,
    out_grad,
):
    owners = lax.axis_size("dp")
    bands = lax.axis_size("mp")
    owner_id = lax.axis_index("dp").astype(I32)
    band_id = lax.axis_index("mp").astype(I32)
    samples, max_cams, _ = visible.shape
    slots, quarter, depth = images.shape
    channels = neck_weight.shape[1]
    queries = bev_query.shape[0]
    rows = slots * quarter
    flat_images = images.reshape(rows, depth)
    lanes, owner = call(
        pack_kernel,
        (
            jax.ShapeDtypeStruct((owners * quarter, 2 * channels), BF16),
            jax.ShapeDtypeStruct((8, slots), I32),
        ),
        owner_id[None],
        cams.reshape(-1, min(128, cams.shape[0])),
        pack[None],
        flat_images,
        cam_keys.reshape(rows, channels),
        neck_weight,
        specs=[smem()] + [vmem()] * 2 + [pl.BlockSpec(memory_space=pl.ANY)] * 3,
        scratch=[
            pltpu.VMEM((rows, depth), BF16),
            pltpu.VMEM((rows, channels), BF16),
            pltpu.VMEM((depth, channels), BF16),
            pltpu.SemaphoreType.DMA((3,)),
        ],
        pinned=False,
    )
    got = lax.all_to_all(
        lanes.reshape(owners, quarter, 2 * channels), "dp", split_axis=0, concat_axis=0, tiled=True
    )
    cost = 1 << 30, 1 << 22
    chips = Y_CHIPS
    deep = owners // (CORES * chips)
    share = depth // (owners * bands)
    lanes_wide = min(128, rows)
    turned = call(
        functools.partial(turn_kernel, chips=chips, depth=deep, bands=bands, share=share),
        on_chip((depth, rows), BF16),
        flat_images,
        scratch=[pltpu.VMEM((rows // lanes_wide, depth, lanes_wide), F32)],
        cost=cost,
    )
    base = call(
        temporal_kernel,
        on_chip((samples, queries, channels), F32),
        band_id[None],
        bev_query,
        point_weight,
        prev_bev,
        align,
        specs=[smem()] + [vmem()] * 4,
        cost=cost,
    )
    first = owner_id * samples
    sample_ids = jnp.arange(cams.shape[0], dtype=I32)
    start = jnp.sum(jnp.where(sample_ids < first, cams, 0))
    local = lax.dynamic_slice(cams, (first,), (samples,))
    window = samples * max_cams
    padded = jnp.concatenate([pack, jnp.zeros((window,), I32)])
    bins = lax.dynamic_slice(padded, (start,), (window,)) // slots
    member = jnp.arange(samples, dtype=I32)
    offset = jnp.sum(jnp.where(member[None, :] < member[:, None], local[None, :], 0), axis=1)
    camera = jnp.arange(max_cams, dtype=I32)
    seen = (visible > 0).astype(I32)
    earlier = (camera[:, None] < camera[None, :]).astype(I32)
    rank = jnp.sum(seen[:, :, None, :] * earlier[None, :, :, None], axis=1)
    place = jnp.arange(SEEN, dtype=I32)
    chosen = (rank[:, :, :, None] == place) & (seen[:, :, :, None] > 0)
    position = jnp.sum(
        jnp.where(chosen, offset[:, None, None, None] + camera[None, :, None, None] + 1, 0), axis=1
    )
    in_window = position[..., None] == jnp.arange(1, window + 1, dtype=I32)
    lane_of = jnp.sum(jnp.where(in_window, bins + 1, 0), axis=-1) - 1
    lane_of = lane_of.transpose(1, 0, 2).reshape(bands * samples * SEEN)
    count = lax.dynamic_slice_in_dim(jnp.sum(seen, axis=1), band_id, 1, axis=1)[:, 0]
    source = jnp.maximum(lane_of, 0)
    got, base, turned, source, count, owner = lax.optimization_barrier(
        (got, base, turned, source, count, owner[0])
    )
    piece = samples * SEEN * quarter
    chosen_kv = call(
        select_kernel,
        on_chip((bands * samples * SEEN, quarter, 2 * channels), BF16),
        source,
        got,
        specs=[smem(), vmem()],
    )
    kv = lax.all_to_all(
        chosen_kv.reshape(bands, piece, 2 * channels), "mp", split_axis=0, concat_axis=0, tiled=True
    )
    bev_out, grads = call(
        attention_kernel,
        (
            jax.ShapeDtypeStruct((samples, queries, channels), BF16),
            on_chip((bands, piece, channels), BF16),
        ),
        count,
        kv,
        base,
        out_grad,
        bev_query,
        norm_gain[None],
        specs=[smem()] + [vmem()] * 5,
    )
    grads = lax.all_to_all(grads, "mp", split_axis=0, concat_axis=0, tiled=True)
    back = call(
        return_kernel,
        on_chip((owners, quarter, channels), BF16),
        source,
        grads.reshape(bands * samples * SEEN, quarter, channels),
        specs=[smem(), vmem()],
        scratch=[pltpu.VMEM((owners, quarter, channels), F32)],
    )
    back = lax.all_to_all(back, "dp", split_axis=0, concat_axis=0, tiled=True)
    neck = call(
        neck_kernel,
        on_chip((depth, channels), F32),
        owner,
        back,
        turned,
        specs=[smem(), vmem(), vmem()],
        scratch=[pltpu.VMEM((rows, channels), BF16)],
    )

    def device(y, z, c):
        return (y * deep + z) * CORES + c

    def exchange(part, axis, groups):
        return lax.all_to_all(
            part, axis, split_axis=0, concat_axis=0, tiled=True, axis_index_groups=groups
        )

    ys, zs, cs = range(chips), range(deep), range(CORES)
    pairs = [[device(y, z, c) for c in cs] for y in ys for z in zs]
    planes = [
        [device(y, z, c) * bands + x for y in ys for x in range(bands)] for z in zs for c in cs
    ]
    columns = [[device(y, z, c) for z in zs] for y in ys for c in cs]
    neck = exchange(neck.reshape(CORES, depth // CORES, channels), "dp", pairs)
    neck = jnp.sum(neck, axis=0).reshape(chips * bands, share * deep, channels)
    neck = exchange(neck, ("dp", "mp"), planes)
    neck = jnp.sum(neck, axis=0).reshape(share, deep, channels).transpose(1, 0, 2)
    neck = exchange(neck, "dp", columns)
    return bev_out, jnp.sum(neck, axis=0) / cams.shape[0]


def solution(mesh):
    return jax.shard_map(
        on_device,
        mesh=mesh,
        in_specs=(
            P(),
            P(),
            P("dp", None, None),
            P("dp", None, "mp"),
            P("dp", "mp", None),
            P("dp", "mp", None),
            P(),
            P("mp", None),
            P("dp", "mp", None),
            P(),
            P(),
            P("dp", "mp", None),
        ),
        out_specs=(P("dp", "mp", None), P(("dp", "mp"), None)),
        check_vma=False,
    )
```

```python
import functools

import jax
import jax.numpy as jnp
from jax import lax
from jax.experimental import pallas as pl
from jax.experimental.pallas import tpu as pltpu
from jax.sharding import PartitionSpec as P

HEADS = 8
KT = 4
CORES = 2
Y_CHIPS = 4
SEEN = 3

NORM_EPS = 1e-05
MASKED = -1e30
BF16 = jnp.bfloat16
F32 = jnp.float32
I32 = jnp.int32


def dot(a, b, a_dim=1, b_dim=0):
    return lax.dot_general(a, b, (((a_dim,), (b_dim,)), ((), ())), preferred_element_type=F32)


def iota(shape, dim):
    return lax.broadcasted_iota(I32, shape, dim)


def vmem():
    return pl.BlockSpec(memory_space=pltpu.VMEM)


def smem():
    return pl.BlockSpec(memory_space=pltpu.SMEM)


def on_chip(shape, dtype):
    return pltpu.VMEM(shape, dtype)


def call(body, outs, *args, specs=None, scratch=(), cost=(1 << 20, 1 << 20), pinned=True):
    specs = specs or [vmem()] * len(args)
    if pinned:
        args = [
            pltpu.with_memory_space_constraint(arg, spec.memory_space) for arg, spec in zip(args, specs)
        ]
    return pl.pallas_call(
        body,
        out_shape=outs,
        in_specs=specs,
        out_specs=jax.tree.map(lambda _: vmem(), outs),
        scratch_shapes=scratch,
        compiler_params=pltpu.CompilerParams(vmem_limit_bytes=24 << 20),
        cost_estimate=pl.CostEstimate(flops=cost[0], bytes_accessed=cost[1], transcendentals=0),
    )(*args)


def pack_kernel(
    bin_ref,
    cams_hbm,
    pack_hbm,
    image_hbm,
    key_hbm,
    weight_hbm,
    lane_ref,
    owner_ref,
    cams_ref,
    pack_ref,
    image_ref,
    key_ref,
    weight_ref,
    feature_ref,
    index_ref,
    sems,
):
    moves = [
        pltpu.make_async_copy(source, target, sems.at[i])
        for i, (source, target) in enumerate(
            (
                (cams_hbm, cams_ref),
                (pack_hbm, pack_ref),
                (image_hbm, image_ref),
                (weight_hbm, weight_ref),
                (key_hbm, key_ref),
            )
        )
    ]
    for move in moves:
        move.start()
    cameras = pack_ref.shape[1]
    rows, channels = key_ref.shape
    slots = owner_ref.shape[1]
    owners, quarter, _ = lane_ref.shape
    groups, width = cams_ref.shape
    spd = groups * width // owners
    lane_ref[...] = jnp.zeros(lane_ref.shape, BF16)
    moves[0].wait()
    first = iota((owners, width), 0) * spd
    before = jnp.zeros((owners, width), F32)
    for g in range(groups):
        counts = cams_ref[g : g + 1, :].astype(F32)
        before += jnp.where(iota((owners, width), 1) + g * width < first, counts, 0.0)
    start = jnp.sum(before, axis=1, keepdims=True)
    moves[1].wait()
    here = (pack_ref[...] - bin_ref[0] * slots) == iota((slots, cameras), 0)
    here = here.astype(F32).astype(BF16)
    number = iota((16, cameras), 1)
    digits = jnp.where(iota((16, cameras), 0) < 8, number // 64, number % 64)
    digits = dot(digits.astype(F32).astype(BF16), here, 1, 1)
    camera = digits[:1] * 64.0 + digits[8:9]
    owner = jnp.sum((start <= camera).astype(F32), axis=0, keepdims=True) - 1.0
    owner_ref[...] = jnp.broadcast_to(owner, owner_ref.shape).astype(I32)
    index = pltpu.make_async_copy(owner_ref, index_ref, sems.at[5])
    index.start()
    moves[2].wait()
    moves[3].wait()
    feature_ref[...] = dot(image_ref[...], weight_ref[...]).astype(BF16)
    index.wait()
    moves[4].wait()
    for s in range(slots):
        here = slice(s * quarter, (s + 1) * quarter)
        lane_ref[index_ref[0, s], :, :channels] = feature_ref[here, :]
        lane_ref[index_ref[0, s], :, channels:] = key_ref[here, :]


def turn_kernel(image_ref, out_ref, turned_ref, *, chips, depth, bands, share):
    turned = image_ref[...].astype(F32).T
    width = turned_ref.shape[2]
    for g in range(turned_ref.shape[0]):
        turned_ref[g] = turned[:, g * width : (g + 1) * width]
    step = CORES * bands * share
    at = 0
    for y in range(chips):
        for c in range(CORES):
            for j in range(bands * share):
                first = y * depth * step + c * bands * share + j
                for g in range(turned_ref.shape[0]):
                    part = turned_ref.at[g][pl.ds(first, depth, stride=step), :]
                    out_ref[at : at + depth, g * width : (g + 1) * width] = part.astype(BF16)
                at += depth


def temporal_kernel(
    band_ref,
    query_ref,
    point_ref,
    prev_ref,
    align_ref,
    cotangent_ref,
    gain_ref,
    base_ref,
    pull_ref,
    heads_ref,
    scale_ref,
):
    samples, cells, channels = prev_ref.shape
    query = query_ref[...]
    head_dim = channels // HEADS
    wide = query.astype(F32)
    gain = gain_ref[...]
    scale_ref[...] = gain
    gates = []
    for k in range(KT):
        shape = (HEADS * KT, channels)
        pick = iota(shape, 0) == (iota(shape, 1) // head_dim) * KT + k
        weight = dot(point_ref[...], pick.astype(F32).astype(BF16)).astype(BF16)
        gates.append(jax.nn.sigmoid(dot(query, weight)))
    for h in range(HEADS):
        mask = (iota((1, channels), 1) // head_dim == h).astype(F32).astype(BF16)
        heads_ref[h * cells : (h + 1) * cells, :] = query * mask
    for m in range(samples):
        total = wide
        for k in range(KT):
            cell = align_ref[m, k : k + 1, :] - band_ref[0] * cells
            pick = (iota((cells, cells), 0) == cell).astype(F32).astype(BF16)
            total = total + gates[k] * dot(pick, prev_ref[m], 0, 0)
        base_ref[m] = total
        pull = cotangent_ref[m].astype(F32) * gain
        pull_ref[m] = pull - jnp.mean(pull, axis=1, keepdims=True)


def select_kernel(source_ref, lane_ref, out_ref):
    for e in range(out_ref.shape[0]):
        out_ref[e] = lane_ref[source_ref[e]]


def attention_kernel(count_ref, kv_ref, base_ref, pull_ref, heads_ref, gain_ref, out_ref, grad_ref):
    parts, rows, width = kv_ref.shape
    samples, queries, channels = base_ref.shape
    step = rows // samples
    keys = parts * step
    head_dim = channels // HEADS
    quarter = step // SEEN
    gain = gain_ref[...]
    lane_head = iota((1, channels), 1) // head_dim
    masks = [(lane_head == h).astype(F32).astype(BF16) for h in range(HEADS)]
    place = iota((keys, HEADS * queries), 0) % step // quarter
    for m in range(samples):
        here = slice(m * step, (m + 1) * step)
        values = kv_ref[:, here, :channels].reshape(keys, channels)
        ray = kv_ref[:, here, channels:].reshape(keys, channels)
        values = jnp.concatenate([values * mask for mask in masks], axis=0)
        scores = dot(ray, heads_ref[...], 1, 1) * (float(head_dim) ** -0.5)
        scores = jnp.where(place < count_ref[m], scores, MASKED)
        raised = jnp.exp(scores - jnp.max(scores, axis=0, keepdims=True))
        probs = (raised * (1.0 / jnp.sum(raised, axis=0, keepdims=True))).astype(BF16)
        tall = jnp.concatenate(
            [probs[:, h * queries : (h + 1) * queries] for h in range(HEADS)], axis=0
        )
        pre_norm = base_ref[m] + dot(tall, values, 0, 0)
        centred = pre_norm - jnp.mean(pre_norm, axis=1, keepdims=True)
        scale = lax.rsqrt(jnp.mean(centred * centred, axis=1, keepdims=True) + NORM_EPS)
        unit = centred * scale
        out_ref[m] = (unit * gain).astype(BF16)
        pull = pull_ref[m]
        pull = pull - unit * jnp.mean(pull * unit, axis=1, keepdims=True)
        pull = (pull * scale).astype(BF16)
        pull = jnp.concatenate([pull * mask for mask in masks], axis=0)
        grad_ref[:, here, :] = dot(probs, pull).astype(BF16).reshape(parts, step, channels)


def return_kernel(source_ref, grad_ref, lane_ref, sum_ref):
    sum_ref[...] = jnp.zeros(sum_ref.shape, F32)
    for e in range(grad_ref.shape[0]):
        lane = source_ref[e]
        sum_ref[lane] = sum_ref[lane] + grad_ref[e].astype(F32)
    lane_ref[...] = sum_ref[...].astype(BF16)


def neck_kernel(owner_ref, lane_ref, turned_ref, out_ref, grad_ref):
    quarter = lane_ref.shape[1]
    for s in range(grad_ref.shape[0] // quarter):
        grad_ref[s * quarter : (s + 1) * quarter, :] = lane_ref[owner_ref[s]]
    out_ref[...] = dot(turned_ref[...], grad_ref[...]).astype(BF16)


def on_device(
    cams,
    pack,
    visible,
    align,
    images,
    cam_keys,
    neck_weight,
    bev_query,
    prev_bev,
    point_weight,
    norm_gain,
    out_grad,
):
    owners = lax.axis_size("dp")
    bands = lax.axis_size("mp")
    owner_id = lax.axis_index("dp").astype(I32)
    band_id = lax.axis_index("mp").astype(I32)
    samples, max_cams, _ = visible.shape
    slots, quarter, depth = images.shape
    channels = neck_weight.shape[1]
    queries = bev_query.shape[0]
    rows = slots * quarter
    flat_images = images.reshape(rows, depth)
    lanes, owner = call(
        pack_kernel,
        (
            jax.ShapeDtypeStruct((owners, quarter, 2 * channels), BF16),
            jax.ShapeDtypeStruct((8, slots), I32),
        ),
        owner_id[None],
        *(
            pltpu.with_memory_space_constraint(arg, pltpu.HBM)
            for arg in (
                cams.reshape(-1, min(128, cams.shape[0])),
                pack[None],
                flat_images,
                cam_keys.reshape(rows, channels),
                neck_weight,
            )
        ),
        specs=[smem()] + [pl.BlockSpec(memory_space=pltpu.HBM)] * 5,
        scratch=[
            pltpu.VMEM((cams.shape[0] // min(128, cams.shape[0]), min(128, cams.shape[0])), I32),
            pltpu.VMEM((1, pack.shape[0]), I32),
            pltpu.VMEM((rows, depth), BF16),
            pltpu.VMEM((rows, channels), BF16),
            pltpu.VMEM((depth, channels), BF16),
            pltpu.VMEM((rows, channels), BF16),
            pltpu.SMEM((8, slots), I32),
            pltpu.SemaphoreType.DMA((6,)),
        ],
        pinned=False,
    )
    got = lax.all_to_all(lanes, "dp", split_axis=0, concat_axis=0, tiled=True)
    cost = 1 << 30, 1 << 22
    chips = Y_CHIPS
    deep = owners // (CORES * chips)
    share = depth // (owners * bands)
    lanes_wide = min(128, rows)
    turned = call(
        functools.partial(turn_kernel, chips=chips, depth=deep, bands=bands, share=share),
        on_chip((depth, rows), BF16),
        flat_images,
        scratch=[pltpu.VMEM((rows // lanes_wide, depth, lanes_wide), F32)],
        cost=cost,
    )
    base, pull, heads, gain = call(
        temporal_kernel,
        (
            on_chip((samples, queries, channels), F32),
            on_chip((samples, queries, channels), F32),
            on_chip((HEADS * queries, channels), BF16),
            on_chip((1, channels), F32),
        ),
        band_id[None],
        bev_query,
        point_weight,
        prev_bev,
        align,
        out_grad,
        norm_gain[None],
        specs=[smem()] + [vmem()] * 6,
        cost=cost,
    )
    first = owner_id * samples
    sample_ids = jnp.arange(cams.shape[0], dtype=I32)
    start = jnp.sum(jnp.where(sample_ids < first, cams, 0))
    local = lax.dynamic_slice(cams, (first,), (samples,))
    window = samples * max_cams
    padded = jnp.concatenate([pack, jnp.zeros((window,), I32)])
    bins = lax.dynamic_slice(padded, (start,), (window,)) // slots
    member = jnp.arange(samples, dtype=I32)
    offset = jnp.sum(jnp.where(member[None, :] < member[:, None], local[None, :], 0), axis=1)
    camera = jnp.arange(max_cams, dtype=I32)
    seen = (visible > 0).astype(I32)
    earlier = (camera[:, None] < camera[None, :]).astype(I32)
    rank = jnp.sum(seen[:, :, None, :] * earlier[None, :, :, None], axis=1)
    place = jnp.arange(SEEN, dtype=I32)
    chosen = (rank[:, :, :, None] == place) & (seen[:, :, :, None] > 0)
    position = jnp.sum(
        jnp.where(chosen, offset[:, None, None, None] + camera[None, :, None, None] + 1, 0), axis=1
    )
    in_window = position[..., None] == jnp.arange(1, window + 1, dtype=I32)
    lane_of = jnp.sum(jnp.where(in_window, bins + 1, 0), axis=-1) - 1
    lane_of = lane_of.transpose(1, 0, 2).reshape(bands * samples * SEEN)
    count = lax.dynamic_slice_in_dim(jnp.sum(seen, axis=1), band_id, 1, axis=1)[:, 0]
    source = jnp.maximum(lane_of, 0)
    got, base, pull, heads, gain, turned, source, count, owner = lax.optimization_barrier(
        (got, base, pull, heads, gain, turned, source, count, owner[0])
    )
    piece = samples * SEEN * quarter
    chosen_kv = call(
        select_kernel,
        on_chip((bands * samples * SEEN, quarter, 2 * channels), BF16),
        source,
        got,
        specs=[smem(), vmem()],
    )
    kv = lax.all_to_all(
        chosen_kv.reshape(bands, piece, 2 * channels), "mp", split_axis=0, concat_axis=0, tiled=True
    )
    bev_out, grads = call(
        attention_kernel,
        (
            jax.ShapeDtypeStruct((samples, queries, channels), BF16),
            on_chip((bands, piece, channels), BF16),
        ),
        count,
        kv,
        base,
        pull,
        heads,
        gain,
        specs=[smem()] + [vmem()] * 5,
    )
    grads = lax.all_to_all(grads, "mp", split_axis=0, concat_axis=0, tiled=True)
    back = call(
        return_kernel,
        on_chip((owners, quarter, channels), BF16),
        source,
        grads.reshape(bands * samples * SEEN, quarter, channels),
        specs=[smem(), vmem()],
        scratch=[pltpu.VMEM((owners, quarter, channels), F32)],
    )
    back = lax.all_to_all(back, "dp", split_axis=0, concat_axis=0, tiled=True)
    neck = call(
        neck_kernel,
        on_chip((depth, channels), BF16),
        owner,
        back,
        turned,
        specs=[smem(), vmem(), vmem()],
        scratch=[pltpu.VMEM((rows, channels), BF16)],
    )

    def device(y, z, c):
        return (y * deep + z) * CORES + c

    def exchange(part, axis, groups):
        return lax.all_to_all(
            part, axis, split_axis=0, concat_axis=0, tiled=True, axis_index_groups=groups
        )

    ys, zs, cs = range(chips), range(deep), range(CORES)
    planes = [
        [device(y, z, c) * bands + x for y in ys for c in cs for x in range(bands)] for z in zs
    ]
    columns = [[device(y, z, c) for z in zs] for y in ys for c in cs]
    neck = neck.reshape(chips * CORES * bands, share * deep, channels)
    neck = exchange(neck, ("dp", "mp"), planes).astype(F32)
    neck = jnp.sum(neck, axis=0).reshape(share, deep, channels).transpose(1, 0, 2)
    neck = exchange(neck, "dp", columns)
    return bev_out, jnp.sum(neck, axis=0) / cams.shape[0]


def solution(mesh):
    return jax.shard_map(
        on_device,
        mesh=mesh,
        in_specs=(
            P(),
            P(),
            P("dp", None, None),
            P("dp", None, "mp"),
            P("dp", "mp", None),
            P("dp", "mp", None),
            P(),
            P("mp", None),
            P("dp", "mp", None),
            P(),
            P(),
            P("dp", "mp", None),
        ),
        out_specs=(P("dp", "mp", None), P(("dp", "mp"), None)),
        check_vma=False,
    )
```

```python
import functools

import jax
import jax.numpy as jnp
from jax import lax
from jax.experimental import pallas as pl
from jax.experimental.pallas import tpu as pltpu
from jax.sharding import PartitionSpec as P

HEADS = 8
KT = 4
CORES = 2
Y_CHIPS = 4
SEEN = 3

NORM_EPS = 1e-05
MASKED = -1e30
LOG2_E = 1.4426950408889634
BF16 = jnp.bfloat16
F32 = jnp.float32
I32 = jnp.int32


def dot(a, b, a_dim=1, b_dim=0):
    return lax.dot_general(a, b, (((a_dim,), (b_dim,)), ((), ())), preferred_element_type=F32)


def iota(shape, dim):
    return lax.broadcasted_iota(I32, shape, dim)


def vmem():
    return pl.BlockSpec(memory_space=pltpu.VMEM)


def smem():
    return pl.BlockSpec(memory_space=pltpu.SMEM)


def on_chip(shape, dtype):
    return pltpu.VMEM(shape, dtype)


def call(body, outs, *args, specs=None, scratch=(), cost=(1 << 20, 1 << 20), pinned=True):
    specs = specs or [vmem()] * len(args)
    if pinned:
        args = [
            pltpu.with_memory_space_constraint(arg, spec.memory_space) for arg, spec in zip(args, specs)
        ]
    return pl.pallas_call(
        body,
        out_shape=outs,
        in_specs=specs,
        out_specs=jax.tree.map(lambda _: vmem(), outs),
        scratch_shapes=scratch,
        compiler_params=pltpu.CompilerParams(vmem_limit_bytes=24 << 20),
        cost_estimate=pl.CostEstimate(flops=cost[0], bytes_accessed=cost[1], transcendentals=0),
    )(*args)


def pack_kernel(
    bin_ref,
    cams_hbm,
    pack_hbm,
    image_hbm,
    key_hbm,
    weight_hbm,
    lane_ref,
    owner_ref,
    cams_ref,
    pack_ref,
    image_ref,
    key_ref,
    weight_ref,
    feature_ref,
    index_ref,
    sems,
):
    moves = [
        pltpu.make_async_copy(source, target, sems.at[i])
        for i, (source, target) in enumerate(
            (
                (cams_hbm, cams_ref),
                (pack_hbm, pack_ref),
                (image_hbm, image_ref),
                (weight_hbm, weight_ref),
                (key_hbm, key_ref),
            )
        )
    ]
    for move in moves:
        move.start()
    cameras = pack_ref.shape[1]
    rows, channels = key_ref.shape
    slots = owner_ref.shape[1]
    owners, quarter, _ = lane_ref.shape
    groups, width = cams_ref.shape
    spd = groups * width // owners
    lane_ref[...] = jnp.zeros(lane_ref.shape, BF16)
    moves[0].wait()
    first = iota((owners, width), 0) * spd
    before = jnp.zeros((owners, width), F32)
    for g in range(groups):
        counts = cams_ref[g : g + 1, :].astype(F32)
        before += jnp.where(iota((owners, width), 1) + g * width < first, counts, 0.0)
    start = jnp.sum(before, axis=1, keepdims=True)
    moves[1].wait()
    here = (pack_ref[...] - bin_ref[0] * slots) == iota((slots, cameras), 0)
    here = here.astype(F32).astype(BF16)
    number = iota((16, cameras), 1)
    digits = jnp.where(iota((16, cameras), 0) < 8, number // 64, number % 64)
    digits = dot(digits.astype(F32).astype(BF16), here, 1, 1)
    camera = digits[:1] * 64.0 + digits[8:9]
    owner = jnp.sum((start <= camera).astype(F32), axis=0, keepdims=True) - 1.0
    owner_ref[...] = jnp.broadcast_to(owner, owner_ref.shape).astype(I32)
    index = pltpu.make_async_copy(owner_ref, index_ref, sems.at[5])
    index.start()
    moves[2].wait()
    moves[3].wait()
    feature_ref[...] = dot(image_ref[...], weight_ref[...]).astype(BF16)
    index.wait()
    moves[4].wait()
    for s in range(slots):
        here = slice(s * quarter, (s + 1) * quarter)
        lane_ref[index_ref[0, s], :, :channels] = feature_ref[here, :]
        lane_ref[index_ref[0, s], :, channels:] = key_ref[here, :]


def turn_kernel(image_ref, out_ref, turned_ref, *, chips, depth, bands, share):
    turned = image_ref[...].astype(F32).T
    width = turned_ref.shape[2]
    for g in range(turned_ref.shape[0]):
        turned_ref[g] = turned[:, g * width : (g + 1) * width]
    step = CORES * bands * share
    at = 0
    for y in range(chips):
        for c in range(CORES):
            for j in range(bands * share):
                first = y * depth * step + c * bands * share + j
                for g in range(turned_ref.shape[0]):
                    part = turned_ref.at[g][pl.ds(first, depth, stride=step), :]
                    out_ref[at : at + depth, g * width : (g + 1) * width] = part.astype(BF16)
                at += depth


def temporal_kernel(
    band_ref,
    query_ref,
    point_ref,
    prev_ref,
    align_ref,
    cotangent_ref,
    gain_ref,
    base_ref,
    pull_ref,
    heads_ref,
    scale_ref,
):
    samples, cells, channels = prev_ref.shape
    query = query_ref[...]
    head_dim = channels // HEADS
    wide = query.astype(F32)
    gain = gain_ref[...]
    scale_ref[...] = gain
    gates = []
    for k in range(KT):
        shape = (HEADS * KT, channels)
        pick = iota(shape, 0) == (iota(shape, 1) // head_dim) * KT + k
        weight = dot(point_ref[...], pick.astype(F32).astype(BF16)).astype(BF16)
        gates.append(jax.nn.sigmoid(dot(query, weight)))
    for h in range(HEADS):
        mask = (iota((1, channels), 1) // head_dim == h).astype(F32).astype(BF16)
        heads_ref[h * cells : (h + 1) * cells, :] = query * mask
    for m in range(samples):
        total = wide
        for k in range(KT):
            cell = align_ref[m, k : k + 1, :] - band_ref[0] * cells
            pick = (iota((cells, cells), 0) == cell).astype(F32).astype(BF16)
            total = total + gates[k] * dot(pick, prev_ref[m], 0, 0)
        base_ref[m] = total
        pull = cotangent_ref[m].astype(F32) * gain
        pull_ref[m] = pull - jnp.mean(pull, axis=1, keepdims=True)


def select_kernel(source_ref, lane_ref, out_ref):
    for e in range(out_ref.shape[0]):
        out_ref[e] = lane_ref[source_ref[e]]


def attention_kernel(
    count_ref,
    kv_ref,
    base_ref,
    pull_ref,
    heads_ref,
    gain_ref,
    out_ref,
    grad_ref,
    score_ref,
    prob_ref,
    norm_ref,
    cross_ref,
):
    parts, rows, width = kv_ref.shape
    samples, queries, channels = base_ref.shape
    step = rows // samples
    keys = parts * step
    head_dim = channels // HEADS
    quarter = step // SEEN
    gain = gain_ref[...]
    lane_head = iota((1, channels), 1) // head_dim
    masks = [(lane_head == h).astype(F32).astype(BF16) for h in range(HEADS)]
    factor = float(head_dim) ** -0.5 * LOG2_E
    place = iota((keys, HEADS * queries), 0) % step // quarter
    spans = [slice(m * step, (m + 1) * step) for m in range(samples)]
    ray = kv_ref[:, :, channels:].reshape(parts * rows, channels)
    score_ref[...] = dot(ray, heads_ref[...], 1, 1).reshape(score_ref.shape)
    for m in range(samples):
        scores = score_ref[:, spans[m], :].reshape(keys, HEADS * queries)
        scores = jnp.where(place < count_ref[m], scores, MASKED)
        raised = jnp.exp2((scores - jnp.max(scores, axis=0, keepdims=True)) * factor)
        prob_ref[m] = (raised * (1.0 / jnp.sum(raised, axis=0, keepdims=True))).astype(BF16)
    for m in range(samples):
        values = kv_ref[:, spans[m], :channels].reshape(keys, channels)
        values = jnp.concatenate([values * mask for mask in masks], axis=0)
        probs = prob_ref[m]
        tall = jnp.concatenate(
            [probs[:, h * queries : (h + 1) * queries] for h in range(HEADS)], axis=0
        )
        norm_ref[m] = base_ref[m] + dot(tall, values, 0, 0)
    for m in range(samples):
        pre_norm = norm_ref[m]
        centred = pre_norm - jnp.mean(pre_norm, axis=1, keepdims=True)
        scale = lax.rsqrt(jnp.mean(centred * centred, axis=1, keepdims=True) + NORM_EPS)
        unit = centred * scale
        out_ref[m] = (unit * gain).astype(BF16)
        pull = pull_ref[m]
        pull = pull - unit * jnp.mean(pull * unit, axis=1, keepdims=True)
        cross_ref[m] = (pull * scale).astype(BF16)
    for m in range(samples):
        pull = cross_ref[m]
        pull = jnp.concatenate([pull * mask for mask in masks], axis=0)
        grad_ref[:, spans[m], :] = dot(prob_ref[m], pull).astype(BF16).reshape(parts, step, channels)


def return_kernel(source_ref, grad_ref, lane_ref, sum_ref):
    sum_ref[...] = jnp.zeros(sum_ref.shape, F32)
    for e in range(grad_ref.shape[0]):
        lane = source_ref[e]
        sum_ref[lane] = sum_ref[lane] + grad_ref[e].astype(F32)
    lane_ref[...] = sum_ref[...].astype(BF16)


def neck_kernel(owner_ref, lane_ref, turned_ref, out_ref, grad_ref, *, samples):
    quarter = lane_ref.shape[1]
    for s in range(grad_ref.shape[0] // quarter):
        grad_ref[s * quarter : (s + 1) * quarter, :] = lane_ref[owner_ref[s]]
    out_ref[...] = (dot(turned_ref[...], grad_ref[...]) * (1.0 / samples)).astype(BF16)


def on_device(
    cams,
    pack,
    visible,
    align,
    images,
    cam_keys,
    neck_weight,
    bev_query,
    prev_bev,
    point_weight,
    norm_gain,
    out_grad,
):
    owners = lax.axis_size("dp")
    bands = lax.axis_size("mp")
    owner_id = lax.axis_index("dp").astype(I32)
    band_id = lax.axis_index("mp").astype(I32)
    samples, max_cams, _ = visible.shape
    slots, quarter, depth = images.shape
    channels = neck_weight.shape[1]
    queries = bev_query.shape[0]
    rows = slots * quarter
    flat_images = images.reshape(rows, depth)
    lanes, owner = call(
        pack_kernel,
        (
            jax.ShapeDtypeStruct((owners, quarter, 2 * channels), BF16),
            jax.ShapeDtypeStruct((8, slots), I32),
        ),
        owner_id[None],
        *(
            pltpu.with_memory_space_constraint(arg, pltpu.HBM)
            for arg in (
                cams.reshape(-1, min(128, cams.shape[0])),
                pack[None],
                flat_images,
                cam_keys.reshape(rows, channels),
                neck_weight,
            )
        ),
        specs=[smem()] + [pl.BlockSpec(memory_space=pltpu.HBM)] * 5,
        scratch=[
            pltpu.VMEM((cams.shape[0] // min(128, cams.shape[0]), min(128, cams.shape[0])), I32),
            pltpu.VMEM((1, pack.shape[0]), I32),
            pltpu.VMEM((rows, depth), BF16),
            pltpu.VMEM((rows, channels), BF16),
            pltpu.VMEM((depth, channels), BF16),
            pltpu.VMEM((rows, channels), BF16),
            pltpu.SMEM((8, slots), I32),
            pltpu.SemaphoreType.DMA((6,)),
        ],
        pinned=False,
    )
    got = lax.all_to_all(lanes, "dp", split_axis=0, concat_axis=0, tiled=True)
    cost = 1 << 30, 1 << 22
    chips = Y_CHIPS
    deep = owners // (CORES * chips)
    share = depth // (owners * bands)
    lanes_wide = min(128, rows)
    turned = call(
        functools.partial(turn_kernel, chips=chips, depth=deep, bands=bands, share=share),
        on_chip((depth, rows), BF16),
        flat_images,
        scratch=[pltpu.VMEM((rows // lanes_wide, depth, lanes_wide), F32)],
        cost=cost,
    )
    base, pull, heads, gain = call(
        temporal_kernel,
        (
            on_chip((samples, queries, channels), F32),
            on_chip((samples, queries, channels), F32),
            on_chip((HEADS * queries, channels), BF16),
            on_chip((1, channels), F32),
        ),
        band_id[None],
        bev_query,
        point_weight,
        prev_bev,
        align,
        out_grad,
        norm_gain[None],
        specs=[smem()] + [vmem()] * 6,
        cost=cost,
    )
    first = owner_id * samples
    sample_ids = jnp.arange(cams.shape[0], dtype=I32)
    start = jnp.sum(jnp.where(sample_ids < first, cams, 0))
    local = lax.dynamic_slice(cams, (first,), (samples,))
    window = samples * max_cams
    padded = jnp.concatenate([pack, jnp.zeros((window,), I32)])
    bins = lax.dynamic_slice(padded, (start,), (window,)) // slots
    member = jnp.arange(samples, dtype=I32)
    offset = jnp.sum(jnp.where(member[None, :] < member[:, None], local[None, :], 0), axis=1)
    camera = jnp.arange(max_cams, dtype=I32)
    seen = (visible > 0).astype(I32)
    earlier = (camera[:, None] < camera[None, :]).astype(I32)
    rank = jnp.sum(seen[:, :, None, :] * earlier[None, :, :, None], axis=1)
    place = jnp.arange(SEEN, dtype=I32)
    chosen = (rank[:, :, :, None] == place) & (seen[:, :, :, None] > 0)
    position = jnp.sum(
        jnp.where(chosen, offset[:, None, None, None] + camera[None, :, None, None] + 1, 0), axis=1
    )
    in_window = position[..., None] == jnp.arange(1, window + 1, dtype=I32)
    lane_of = jnp.sum(jnp.where(in_window, bins + 1, 0), axis=-1) - 1
    lane_of = lane_of.transpose(1, 0, 2).reshape(bands * samples * SEEN)
    count = lax.dynamic_slice_in_dim(jnp.sum(seen, axis=1), band_id, 1, axis=1)[:, 0]
    source = jnp.maximum(lane_of, 0)
    got, base, pull, heads, gain, turned, source, count, owner = lax.optimization_barrier(
        (got, base, pull, heads, gain, turned, source, count, owner[0])
    )
    piece = samples * SEEN * quarter
    chosen_kv = call(
        select_kernel,
        on_chip((bands * samples * SEEN, quarter, 2 * channels), BF16),
        source,
        got,
        specs=[smem(), vmem()],
    )
    kv = lax.all_to_all(
        chosen_kv.reshape(bands, piece, 2 * channels), "mp", split_axis=0, concat_axis=0, tiled=True
    )
    bev_out, grads = call(
        attention_kernel,
        (
            jax.ShapeDtypeStruct((samples, queries, channels), BF16),
            on_chip((bands, piece, channels), BF16),
        ),
        count,
        kv,
        base,
        pull,
        heads,
        gain,
        specs=[smem()] + [vmem()] * 5,
        scratch=[
            pltpu.VMEM((bands, piece, HEADS * queries), F32),
            pltpu.VMEM((samples, bands * SEEN * quarter, HEADS * queries), BF16),
            pltpu.VMEM((samples, queries, channels), F32),
            pltpu.VMEM((samples, queries, channels), BF16),
        ],
    )
    grads = lax.all_to_all(grads, "mp", split_axis=0, concat_axis=0, tiled=True)
    back = call(
        return_kernel,
        on_chip((owners, quarter, channels), BF16),
        source,
        grads.reshape(bands * samples * SEEN, quarter, channels),
        specs=[smem(), vmem()],
        scratch=[pltpu.VMEM((owners, quarter, channels), F32)],
    )
    back = lax.all_to_all(back, "dp", split_axis=0, concat_axis=0, tiled=True)
    neck = call(
        functools.partial(neck_kernel, samples=cams.shape[0]),
        on_chip((depth, channels), BF16),
        owner,
        back,
        turned,
        specs=[smem(), vmem(), vmem()],
        scratch=[pltpu.VMEM((rows, channels), BF16)],
    )

    def device(y, z, c):
        return (y * deep + z) * CORES + c

    def exchange(part, axis, groups):
        return lax.all_to_all(
            part, axis, split_axis=0, concat_axis=0, tiled=True, axis_index_groups=groups
        )

    ys, zs, cs = range(chips), range(deep), range(CORES)
    planes = [
        [device(y, z, c) * bands + x for y in ys for c in cs for x in range(bands)] for z in zs
    ]
    columns = [[device(y, z, c) for z in zs] for y in ys for c in cs]
    neck = neck.reshape(chips * CORES * bands, share * deep, channels)
    neck = exchange(neck, ("dp", "mp"), planes).astype(F32)
    neck = jnp.sum(neck, axis=0).reshape(share, deep, channels).transpose(1, 0, 2)
    neck = exchange(neck, "dp", columns)
    return bev_out, jnp.sum(neck, axis=0)


def solution(mesh):
    return jax.shard_map(
        on_device,
        mesh=mesh,
        in_specs=(
            P(),
            P(),
            P("dp", None, None),
            P("dp", None, "mp"),
            P("dp", "mp", None),
            P("dp", "mp", None),
            P(),
            P("mp", None),
            P("dp", "mp", None),
            P(),
            P(),
            P("dp", "mp", None),
        ),
        out_specs=(P("dp", "mp", None), P(("dp", "mp"), None)),
        check_vma=False,
    )
```

```python
import functools

import jax
import jax.numpy as jnp
from jax import lax
from jax.experimental import pallas as pl
from jax.experimental.pallas import tpu as pltpu
from jax.sharding import PartitionSpec as P

HEADS = 8
KT = 4
CORES = 2
Y_CHIPS = 4
SEEN = 3

NORM_EPS = 1e-05
MASKED = -1e30
LOG2_E = 1.4426950408889634
BF16 = jnp.bfloat16
F32 = jnp.float32
I32 = jnp.int32


def dot(a, b, a_dim=1, b_dim=0):
    return lax.dot_general(a, b, (((a_dim,), (b_dim,)), ((), ())), preferred_element_type=F32)


def iota(shape, dim):
    return lax.broadcasted_iota(I32, shape, dim)


def vmem():
    return pl.BlockSpec(memory_space=pltpu.VMEM)


def smem():
    return pl.BlockSpec(memory_space=pltpu.SMEM)


def on_chip(shape, dtype):
    return pltpu.VMEM(shape, dtype)


def call(body, outs, *args, specs=None, scratch=(), cost=(1 << 20, 1 << 20), pinned=True):
    specs = specs or [vmem()] * len(args)
    if pinned:
        args = [
            pltpu.with_memory_space_constraint(arg, spec.memory_space) for arg, spec in zip(args, specs)
        ]
    return pl.pallas_call(
        body,
        out_shape=outs,
        in_specs=specs,
        out_specs=jax.tree.map(lambda _: vmem(), outs),
        scratch_shapes=scratch,
        compiler_params=pltpu.CompilerParams(vmem_limit_bytes=24 << 20),
        cost_estimate=pl.CostEstimate(flops=cost[0], bytes_accessed=cost[1], transcendentals=0),
    )(*args)


def pack_kernel(
    bin_ref,
    cams_hbm,
    pack_hbm,
    image_hbm,
    key_hbm,
    weight_hbm,
    lane_ref,
    owner_ref,
    cams_ref,
    pack_ref,
    image_ref,
    key_ref,
    weight_ref,
    feature_ref,
    index_ref,
    sems,
):
    moves = [
        pltpu.make_async_copy(source, target, sems.at[i])
        for i, (source, target) in enumerate(
            (
                (cams_hbm, cams_ref),
                (pack_hbm, pack_ref),
                (image_hbm, image_ref),
                (weight_hbm, weight_ref),
                (key_hbm, key_ref),
            )
        )
    ]
    for move in moves:
        move.start()
    cameras = pack_ref.shape[1]
    rows, channels = key_ref.shape
    slots = owner_ref.shape[1]
    owners, quarter, _ = lane_ref.shape
    groups, width = cams_ref.shape
    spd = groups * width // owners
    lane_ref[...] = jnp.zeros(lane_ref.shape, BF16)
    moves[0].wait()
    first = iota((owners, width), 0) * spd
    before = jnp.zeros((owners, width), F32)
    for g in range(groups):
        counts = cams_ref[g : g + 1, :].astype(F32)
        before += jnp.where(iota((owners, width), 1) + g * width < first, counts, 0.0)
    start = jnp.sum(before, axis=1, keepdims=True)
    moves[1].wait()
    here = (pack_ref[...] - bin_ref[0] * slots) == iota((slots, cameras), 0)
    here = here.astype(F32).astype(BF16)
    number = iota((16, cameras), 1)
    digits = jnp.where(iota((16, cameras), 0) < 8, number // 64, number % 64)
    digits = dot(digits.astype(F32).astype(BF16), here, 1, 1)
    camera = digits[:1] * 64.0 + digits[8:9]
    owner = jnp.sum((start <= camera).astype(F32), axis=0, keepdims=True) - 1.0
    owner_ref[...] = jnp.broadcast_to(owner, owner_ref.shape).astype(I32)
    index = pltpu.make_async_copy(owner_ref, index_ref, sems.at[5])
    index.start()
    moves[2].wait()
    moves[3].wait()
    feature_ref[...] = dot(image_ref[...], weight_ref[...]).astype(BF16)
    index.wait()
    moves[4].wait()
    for s in range(slots):
        here = slice(s * quarter, (s + 1) * quarter)
        lane_ref[index_ref[0, s], :, :channels] = feature_ref[here, :]
        lane_ref[index_ref[0, s], :, channels:] = key_ref[here, :]


def deal_kernel(lane_ref, image_ref, out_ref):
    quarter = out_ref.shape[1]
    out_ref[...] = jnp.zeros(out_ref.shape, BF16)
    for s in range(image_ref.shape[0] // quarter):
        out_ref[lane_ref[s]] = image_ref[s * quarter : (s + 1) * quarter, :]


def turn_kernel(*refs, bands, share):
    out_ref, block_ref, turned_ref = refs[-3:]
    pieces = refs[:-3]
    deep, quarter, _ = pieces[0].shape
    for z in range(deep):
        for p, piece in enumerate(pieces):
            at = (z * len(pieces) + p) * quarter
            block_ref[at : at + quarter, :] = piece[z]
    groups, _, width = turned_ref.shape
    for g in range(groups):
        turned_ref[g] = block_ref[g * width : (g + 1) * width, :].astype(F32).T
    step = CORES * bands * share
    at = 0
    for y in range(len(pieces) // CORES):
        for c in range(CORES):
            for j in range(bands * share):
                first = y * deep * step + c * bands * share + j
                for g in range(groups):
                    part = turned_ref.at[g][pl.ds(first, deep, stride=step), :]
                    out_ref[at : at + deep, g * width : (g + 1) * width] = part.astype(BF16)
                at += deep


def temporal_kernel(
    band_ref,
    query_ref,
    point_ref,
    prev_ref,
    align_ref,
    cotangent_ref,
    gain_ref,
    base_ref,
    pull_ref,
    heads_ref,
    scale_ref,
):
    samples, cells, channels = prev_ref.shape
    query = query_ref[...]
    head_dim = channels // HEADS
    wide = query.astype(F32)
    gain = gain_ref[...]
    scale_ref[...] = gain
    gates = []
    for k in range(KT):
        shape = (HEADS * KT, channels)
        pick = iota(shape, 0) == (iota(shape, 1) // head_dim) * KT + k
        weight = dot(point_ref[...], pick.astype(F32).astype(BF16)).astype(BF16)
        gates.append(jax.nn.sigmoid(dot(query, weight)))
    for h in range(HEADS):
        mask = (iota((1, channels), 1) // head_dim == h).astype(F32).astype(BF16)
        heads_ref[h * cells : (h + 1) * cells, :] = query * mask
    for m in range(samples):
        total = wide
        for k in range(KT):
            cell = align_ref[m, k : k + 1, :] - band_ref[0] * cells
            pick = (iota((cells, cells), 0) == cell).astype(F32).astype(BF16)
            total = total + gates[k] * dot(pick, prev_ref[m], 0, 0)
        base_ref[m] = total
        pull = cotangent_ref[m].astype(F32) * gain
        pull_ref[m] = pull - jnp.mean(pull, axis=1, keepdims=True)


def select_kernel(source_ref, lane_ref, out_ref):
    for e in range(out_ref.shape[0]):
        out_ref[e] = lane_ref[source_ref[e]]


def attention_kernel(
    count_ref,
    kv_ref,
    base_ref,
    pull_ref,
    heads_ref,
    gain_ref,
    out_ref,
    grad_ref,
    score_ref,
    prob_ref,
    norm_ref,
    cross_ref,
):
    parts, rows, width = kv_ref.shape
    samples, queries, channels = base_ref.shape
    step = rows // samples
    keys = parts * step
    head_dim = channels // HEADS
    quarter = step // SEEN
    gain = gain_ref[...]
    lane_head = iota((1, channels), 1) // head_dim
    masks = [(lane_head == h).astype(F32).astype(BF16) for h in range(HEADS)]
    factor = float(head_dim) ** -0.5 * LOG2_E
    place = iota((keys, HEADS * queries), 0) % step // quarter
    spans = [slice(m * step, (m + 1) * step) for m in range(samples)]
    ray = kv_ref[:, :, channels:].reshape(parts * rows, channels)
    score_ref[...] = dot(ray, heads_ref[...], 1, 1).reshape(score_ref.shape)
    for m in range(samples):
        scores = score_ref[:, spans[m], :].reshape(keys, HEADS * queries)
        scores = jnp.where(place < count_ref[m], scores, MASKED)
        raised = jnp.exp2((scores - jnp.max(scores, axis=0, keepdims=True)) * factor)
        prob_ref[m] = (raised * (1.0 / jnp.sum(raised, axis=0, keepdims=True))).astype(BF16)
    for m in range(samples):
        values = kv_ref[:, spans[m], :channels].reshape(keys, channels)
        values = jnp.concatenate([values * mask for mask in masks], axis=0)
        probs = prob_ref[m]
        tall = jnp.concatenate(
            [probs[:, h * queries : (h + 1) * queries] for h in range(HEADS)], axis=0
        )
        norm_ref[m] = base_ref[m] + dot(tall, values, 0, 0)
    for m in range(samples):
        pre_norm = norm_ref[m]
        centred = pre_norm - jnp.mean(pre_norm, axis=1, keepdims=True)
        scale = lax.rsqrt(jnp.mean(centred * centred, axis=1, keepdims=True) + NORM_EPS)
        unit = centred * scale
        out_ref[m] = (unit * gain).astype(BF16)
        pull = pull_ref[m]
        pull = pull - unit * jnp.mean(pull * unit, axis=1, keepdims=True)
        cross_ref[m] = (pull * scale).astype(BF16)
    for m in range(samples):
        pull = cross_ref[m]
        pull = jnp.concatenate([pull * mask for mask in masks], axis=0)
        grad_ref[:, spans[m], :] = dot(prob_ref[m], pull).astype(BF16).reshape(parts, step, channels)


def return_kernel(source_ref, grad_ref, lane_ref, sum_ref):
    sum_ref[...] = jnp.zeros(sum_ref.shape, F32)
    for e in range(grad_ref.shape[0]):
        lane = source_ref[e]
        sum_ref[lane] = sum_ref[lane] + grad_ref[e].astype(F32)
    lane_ref[...] = sum_ref[...].astype(BF16)


def neck_kernel(grad_ref, turned_ref, out_ref, *, samples):
    out_ref[...] = (dot(turned_ref[...], grad_ref[...]) * (1.0 / samples)).astype(BF16)


def on_device(
    cams,
    pack,
    visible,
    align,
    images,
    cam_keys,
    neck_weight,
    bev_query,
    prev_bev,
    point_weight,
    norm_gain,
    out_grad,
):
    owners = lax.axis_size("dp")
    bands = lax.axis_size("mp")
    owner_id = lax.axis_index("dp").astype(I32)
    band_id = lax.axis_index("mp").astype(I32)
    samples, max_cams, _ = visible.shape
    slots, quarter, depth = images.shape
    channels = neck_weight.shape[1]
    queries = bev_query.shape[0]
    rows = slots * quarter
    flat_images = images.reshape(rows, depth)
    lanes, owner = call(
        pack_kernel,
        (
            jax.ShapeDtypeStruct((owners, quarter, 2 * channels), BF16),
            jax.ShapeDtypeStruct((8, slots), I32),
        ),
        owner_id[None],
        *(
            pltpu.with_memory_space_constraint(arg, pltpu.HBM)
            for arg in (
                cams.reshape(-1, min(128, cams.shape[0])),
                pack[None],
                flat_images,
                cam_keys.reshape(rows, channels),
                neck_weight,
            )
        ),
        specs=[smem()] + [pl.BlockSpec(memory_space=pltpu.HBM)] * 5,
        scratch=[
            pltpu.VMEM((cams.shape[0] // min(128, cams.shape[0]), min(128, cams.shape[0])), I32),
            pltpu.VMEM((1, pack.shape[0]), I32),
            pltpu.VMEM((rows, depth), BF16),
            pltpu.VMEM((rows, channels), BF16),
            pltpu.VMEM((depth, channels), BF16),
            pltpu.VMEM((rows, channels), BF16),
            pltpu.SMEM((8, slots), I32),
            pltpu.SemaphoreType.DMA((6,)),
        ],
        pinned=False,
    )
    got = lax.all_to_all(lanes, "dp", split_axis=0, concat_axis=0, tiled=True)
    cost = 1 << 30, 1 << 22
    chips = Y_CHIPS
    deep = owners // (CORES * chips)
    share = depth // (owners * bands)

    def device(y, z, c):
        return (y * deep + z) * CORES + c

    def place_of(device_id):
        return device_id // (deep * CORES), device_id // CORES % deep, device_id % CORES

    ys, zs, cs = range(chips), range(deep), range(CORES)
    my_y, _, my_core = place_of(owner_id)
    owner_y, owner_z, owner_core = place_of(owner[0])
    column = (owner_y - my_y) % chips * CORES + (owner_core + my_core) % CORES
    dealt = call(
        deal_kernel,
        jax.ShapeDtypeStruct((owners, quarter, depth), BF16),
        column * deep + owner_z,
        flat_images,
        specs=[smem(), vmem()],
        cost=cost,
    ).reshape(chips * CORES, deep, quarter, depth)
    pieces = [dealt[0]]
    for p in range(1, chips * CORES):
        moves = [
            (device(y, z, c), device((y + p // CORES) % chips, z, (c + p) % CORES))
            for y in ys
            for z in zs
            for c in cs
        ]
        pieces.append(lax.ppermute(dealt[p], "dp", moves))
    tokens = owners * quarter
    turned = call(
        functools.partial(turn_kernel, bands=bands, share=share),
        on_chip((depth, tokens), BF16),
        *pieces,
        scratch=[
            pltpu.VMEM((tokens, depth), BF16),
            pltpu.VMEM((tokens // 128, depth, 128), F32),
        ],
        cost=cost,
        pinned=False,
    )
    base, pull, heads, gain = call(
        temporal_kernel,
        (
            on_chip((samples, queries, channels), F32),
            on_chip((samples, queries, channels), F32),
            on_chip((HEADS * queries, channels), BF16),
            on_chip((1, channels), F32),
        ),
        band_id[None],
        bev_query,
        point_weight,
        prev_bev,
        align,
        out_grad,
        norm_gain[None],
        specs=[smem()] + [vmem()] * 6,
        cost=cost,
    )
    first = owner_id * samples
    sample_ids = jnp.arange(cams.shape[0], dtype=I32)
    start = jnp.sum(jnp.where(sample_ids < first, cams, 0))
    local = lax.dynamic_slice(cams, (first,), (samples,))
    window = samples * max_cams
    padded = jnp.concatenate([pack, jnp.zeros((window,), I32)])
    bins = lax.dynamic_slice(padded, (start,), (window,)) // slots
    member = jnp.arange(samples, dtype=I32)
    offset = jnp.sum(jnp.where(member[None, :] < member[:, None], local[None, :], 0), axis=1)
    camera = jnp.arange(max_cams, dtype=I32)
    seen = (visible > 0).astype(I32)
    earlier = (camera[:, None] < camera[None, :]).astype(I32)
    rank = jnp.sum(seen[:, :, None, :] * earlier[None, :, :, None], axis=1)
    place = jnp.arange(SEEN, dtype=I32)
    chosen = (rank[:, :, :, None] == place) & (seen[:, :, :, None] > 0)
    position = jnp.sum(
        jnp.where(chosen, offset[:, None, None, None] + camera[None, :, None, None] + 1, 0), axis=1
    )
    in_window = position[..., None] == jnp.arange(1, window + 1, dtype=I32)
    lane_of = jnp.sum(jnp.where(in_window, bins + 1, 0), axis=-1) - 1
    lane_of = lane_of.transpose(1, 0, 2).reshape(bands * samples * SEEN)
    count = lax.dynamic_slice_in_dim(jnp.sum(seen, axis=1), band_id, 1, axis=1)[:, 0]
    source = jnp.maximum(lane_of, 0)
    bin_y, bin_z, bin_core = place_of(source)
    back_lane = (bin_z * chips + (my_y - bin_y) % chips) * CORES + (bin_core + my_core) % CORES
    got, base, pull, heads, gain, turned, source, back_lane, count = lax.optimization_barrier(
        (got, base, pull, heads, gain, turned, source, back_lane, count)
    )
    piece = samples * SEEN * quarter
    chosen_kv = call(
        select_kernel,
        on_chip((bands * samples * SEEN, quarter, 2 * channels), BF16),
        source,
        got,
        specs=[smem(), vmem()],
    )
    kv = lax.all_to_all(
        chosen_kv.reshape(bands, piece, 2 * channels), "mp", split_axis=0, concat_axis=0, tiled=True
    )
    bev_out, grads = call(
        attention_kernel,
        (
            jax.ShapeDtypeStruct((samples, queries, channels), BF16),
            on_chip((bands, piece, channels), BF16),
        ),
        count,
        kv,
        base,
        pull,
        heads,
        gain,
        specs=[smem()] + [vmem()] * 5,
        scratch=[
            pltpu.VMEM((bands, piece, HEADS * queries), F32),
            pltpu.VMEM((samples, bands * SEEN * quarter, HEADS * queries), BF16),
            pltpu.VMEM((samples, queries, channels), F32),
            pltpu.VMEM((samples, queries, channels), BF16),
        ],
    )
    grads = lax.all_to_all(grads, "mp", split_axis=0, concat_axis=0, tiled=True)
    back = call(
        return_kernel,
        on_chip((owners, quarter, channels), BF16),
        back_lane,
        grads.reshape(bands * samples * SEEN, quarter, channels),
        specs=[smem(), vmem()],
        scratch=[pltpu.VMEM((owners, quarter, channels), F32)],
    )

    def exchange(part, axis, groups):
        return lax.all_to_all(
            part, axis, split_axis=0, concat_axis=0, tiled=True, axis_index_groups=groups
        )

    columns = [[device(y, z, c) for z in zs] for y in ys for c in cs]
    back = exchange(back.reshape(deep, tokens // deep, channels), "dp", columns)
    neck = call(
        functools.partial(neck_kernel, samples=cams.shape[0]),
        on_chip((depth, channels), BF16),
        back.reshape(tokens, channels),
        turned,
    )
    planes = [
        [device(y, z, c) * bands + x for y in ys for c in cs for x in range(bands)] for z in zs
    ]
    neck = neck.reshape(chips * CORES * bands, share * deep, channels)
    neck = exchange(neck, ("dp", "mp"), planes).astype(F32)
    neck = jnp.sum(neck, axis=0).reshape(share, deep, channels).transpose(1, 0, 2)
    neck = exchange(neck, "dp", columns)
    return bev_out, jnp.sum(neck, axis=0)


def solution(mesh):
    return jax.shard_map(
        on_device,
        mesh=mesh,
        in_specs=(
            P(),
            P(),
            P("dp", None, None),
            P("dp", None, "mp"),
            P("dp", "mp", None),
            P("dp", "mp", None),
            P(),
            P("mp", None),
            P("dp", "mp", None),
            P(),
            P(),
            P("dp", "mp", None),
        ),
        out_specs=(P("dp", "mp", None), P(("dp", "mp"), None)),
        check_vma=False,
    )
```

```python
import functools

import jax
import jax.numpy as jnp
from jax import lax
from jax.experimental import pallas as pl
from jax.experimental.pallas import tpu as pltpu
from jax.sharding import PartitionSpec as P

HEADS = 8
KT = 4
CORES = 2
Y_CHIPS = 4
SEEN = 3

NORM_EPS = 1e-05
MASKED = -1e30
LOG2_E = 1.4426950408889634
BF16 = jnp.bfloat16
F32 = jnp.float32
I32 = jnp.int32


def dot(a, b, a_dim=1, b_dim=0):
    return lax.dot_general(a, b, (((a_dim,), (b_dim,)), ((), ())), preferred_element_type=F32)


def iota(shape, dim):
    return lax.broadcasted_iota(I32, shape, dim)


def vmem():
    return pl.BlockSpec(memory_space=pltpu.VMEM)


def smem():
    return pl.BlockSpec(memory_space=pltpu.SMEM)


def on_chip(shape, dtype):
    return pltpu.VMEM(shape, dtype)


def call(body, outs, *args, specs=None, scratch=(), cost=(1 << 20, 1 << 20), pinned=True):
    specs = specs or [vmem()] * len(args)
    if pinned:
        args = [
            pltpu.with_memory_space_constraint(arg, spec.memory_space) for arg, spec in zip(args, specs)
        ]
    return pl.pallas_call(
        body,
        out_shape=outs,
        in_specs=specs,
        out_specs=jax.tree.map(lambda _: vmem(), outs),
        scratch_shapes=scratch,
        compiler_params=pltpu.CompilerParams(vmem_limit_bytes=24 << 20),
        cost_estimate=pl.CostEstimate(flops=cost[0], bytes_accessed=cost[1], transcendentals=0),
    )(*args)


def pack_kernel(
    bin_ref,
    cams_hbm,
    pack_hbm,
    image_hbm,
    key_hbm,
    weight_hbm,
    lane_ref,
    owner_ref,
    cams_ref,
    pack_ref,
    image_ref,
    key_ref,
    weight_ref,
    feature_ref,
    index_ref,
    sems,
):
    moves = [
        pltpu.make_async_copy(source, target, sems.at[i])
        for i, (source, target) in enumerate(
            (
                (cams_hbm, cams_ref),
                (pack_hbm, pack_ref),
                (image_hbm, image_ref),
                (weight_hbm, weight_ref),
                (key_hbm, key_ref),
            )
        )
    ]
    for move in moves:
        move.start()
    cameras = pack_ref.shape[1]
    rows, channels = key_ref.shape
    slots = owner_ref.shape[1]
    owners, quarter, _ = lane_ref.shape
    groups, width = cams_ref.shape
    spd = groups * width // owners
    lane_ref[...] = jnp.zeros(lane_ref.shape, BF16)
    moves[0].wait()
    first = iota((owners, width), 0) * spd
    before = jnp.zeros((owners, width), F32)
    for g in range(groups):
        counts = cams_ref[g : g + 1, :].astype(F32)
        before += jnp.where(iota((owners, width), 1) + g * width < first, counts, 0.0)
    start = jnp.sum(before, axis=1, keepdims=True)
    moves[1].wait()
    here = (pack_ref[...] - bin_ref[0] * slots) == iota((slots, cameras), 0)
    here = here.astype(F32).astype(BF16)
    number = iota((16, cameras), 1)
    digits = jnp.where(iota((16, cameras), 0) < 8, number // 64, number % 64)
    digits = dot(digits.astype(F32).astype(BF16), here, 1, 1)
    camera = digits[:1] * 64.0 + digits[8:9]
    owner = jnp.sum((start <= camera).astype(F32), axis=0, keepdims=True) - 1.0
    owner_ref[...] = jnp.broadcast_to(owner, owner_ref.shape).astype(I32)
    index = pltpu.make_async_copy(owner_ref, index_ref, sems.at[5])
    index.start()
    moves[2].wait()
    moves[3].wait()
    feature_ref[...] = dot(image_ref[...], weight_ref[...]).astype(BF16)
    index.wait()
    moves[4].wait()
    for s in range(slots):
        here = slice(s * quarter, (s + 1) * quarter)
        lane_ref[index_ref[0, s], :, :channels] = feature_ref[here, :]
        lane_ref[index_ref[0, s], :, channels:] = key_ref[here, :]


def deal_kernel(lane_ref, image_ref, out_ref):
    quarter = out_ref.shape[1]
    out_ref[...] = jnp.zeros(out_ref.shape, BF16)
    for s in range(image_ref.shape[0] // quarter):
        out_ref[lane_ref[s]] = image_ref[s * quarter : (s + 1) * quarter, :]


def turn_kernel(*refs, bands, share):
    out_ref, block_ref, turned_ref, sems = refs[-4:]
    pieces = refs[:-4]
    deep, quarter, _ = pieces[0].shape
    moves = [
        pltpu.make_async_copy(piece, block_ref.at[:, p], sems.at[p]) for p, piece in enumerate(pieces)
    ]
    for move in moves:
        move.start()
    for move in moves:
        move.wait()
    groups, depth, width = turned_ref.shape
    some = width // (len(pieces) * quarter)
    for g in range(groups):
        block = block_ref[g * some : (g + 1) * some].reshape(width, depth)
        turned_ref[g] = block.astype(F32).T
    step = CORES * bands * share
    at = 0
    for y in range(len(pieces) // CORES):
        for c in range(CORES):
            for j in range(bands * share):
                first = y * deep * step + c * bands * share + j
                for g in range(groups):
                    part = turned_ref.at[g][pl.ds(first, deep, stride=step), :]
                    out_ref[at : at + deep, g * width : (g + 1) * width] = part.astype(BF16)
                at += deep


def temporal_kernel(
    band_ref,
    query_ref,
    point_ref,
    prev_ref,
    align_ref,
    cotangent_ref,
    gain_ref,
    base_ref,
    pull_ref,
    scale_ref,
):
    samples, cells, channels = prev_ref.shape
    query = query_ref[...]
    head_dim = channels // HEADS
    wide = query.astype(F32)
    gain = gain_ref[...]
    scale_ref[...] = gain
    gates = []
    for k in range(KT):
        shape = (HEADS * KT, channels)
        pick = iota(shape, 0) == (iota(shape, 1) // head_dim) * KT + k
        weight = dot(point_ref[...], pick.astype(F32).astype(BF16)).astype(BF16)
        gates.append(jax.nn.sigmoid(dot(query, weight)))
    for m in range(samples):
        total = wide
        for k in range(KT):
            cell = align_ref[m, k : k + 1, :] - band_ref[0] * cells
            pick = (iota((cells, cells), 0) == cell).astype(F32).astype(BF16)
            total = total + gates[k] * dot(pick, prev_ref[m], 0, 0)
        base_ref[m] = total
        pull = cotangent_ref[m].astype(F32) * gain
        pull_ref[m] = pull - jnp.mean(pull, axis=1, keepdims=True)


def select_kernel(source_ref, lane_ref, out_ref):
    for e in range(out_ref.shape[0]):
        out_ref[e] = lane_ref[source_ref[e]]


def attention_kernel(
    count_ref,
    kv_ref,
    base_hbm,
    pull_hbm,
    query_ref,
    gain_ref,
    out_ref,
    grad_ref,
    base_ref,
    pull_ref,
    sems,
    heads_ref,
    score_ref,
    prob_ref,
    norm_ref,
    cross_ref,
):
    moves = [
        pltpu.make_async_copy(base_hbm, base_ref, sems.at[0]),
        pltpu.make_async_copy(pull_hbm, pull_ref, sems.at[1]),
    ]
    for move in moves:
        move.start()
    parts, rows, width = kv_ref.shape
    samples, queries, channels = base_ref.shape
    step = rows // samples
    keys = parts * step
    head_dim = channels // HEADS
    quarter = step // SEEN
    gain = gain_ref[...]
    lane_head = iota((1, channels), 1) // head_dim
    masks = [(lane_head == h).astype(F32).astype(BF16) for h in range(HEADS)]
    factor = float(head_dim) ** -0.5 * LOG2_E
    place = iota((keys, HEADS * queries), 0) % step // quarter
    for h in range(HEADS):
        heads_ref[h * queries : (h + 1) * queries, :] = query_ref[...] * masks[h]
    spans = [slice(m * step, (m + 1) * step) for m in range(samples)]
    ray = kv_ref[:, :, channels:].reshape(parts * rows, channels)
    score_ref[...] = dot(ray, heads_ref[...], 1, 1).reshape(score_ref.shape)
    for m in range(samples):
        scores = score_ref[:, spans[m], :].reshape(keys, HEADS * queries)
        scores = jnp.where(place < count_ref[m], scores, MASKED)
        raised = jnp.exp2((scores - jnp.max(scores, axis=0, keepdims=True)) * factor)
        prob_ref[m] = (raised * (1.0 / jnp.sum(raised, axis=0, keepdims=True))).astype(BF16)
    moves[0].wait()
    for m in range(samples):
        values = kv_ref[:, spans[m], :channels].reshape(keys, channels)
        values = jnp.concatenate([values * mask for mask in masks], axis=0)
        probs = prob_ref[m]
        tall = jnp.concatenate(
            [probs[:, h * queries : (h + 1) * queries] for h in range(HEADS)], axis=0
        )
        norm_ref[m] = base_ref[m] + dot(tall, values, 0, 0)
    moves[1].wait()
    for m in range(samples):
        pre_norm = norm_ref[m]
        centred = pre_norm - jnp.mean(pre_norm, axis=1, keepdims=True)
        scale = lax.rsqrt(jnp.mean(centred * centred, axis=1, keepdims=True) + NORM_EPS)
        unit = centred * scale
        out_ref[m] = (unit * gain).astype(BF16)
        pull = pull_ref[m]
        pull = pull - unit * jnp.mean(pull * unit, axis=1, keepdims=True)
        cross_ref[m] = (pull * scale).astype(BF16)
    for m in range(samples):
        pull = cross_ref[m]
        pull = jnp.concatenate([pull * mask for mask in masks], axis=0)
        grad_ref[:, spans[m], :] = dot(prob_ref[m], pull).astype(BF16).reshape(parts, step, channels)


def return_kernel(source_ref, grad_ref, lane_ref, sum_ref):
    sum_ref[...] = jnp.zeros(sum_ref.shape, F32)
    for e in range(grad_ref.shape[0]):
        lane = source_ref[e]
        sum_ref[lane] = sum_ref[lane] + grad_ref[e].astype(F32)
    lane_ref[...] = sum_ref[...].astype(BF16)


def neck_kernel(grad_ref, turned_ref, out_ref, *, samples):
    out_ref[...] = (dot(turned_ref[...], grad_ref[...]) * (1.0 / samples)).astype(BF16)


def on_device(
    cams,
    pack,
    visible,
    align,
    images,
    cam_keys,
    neck_weight,
    bev_query,
    prev_bev,
    point_weight,
    norm_gain,
    out_grad,
):
    owners = lax.axis_size("dp")
    bands = lax.axis_size("mp")
    owner_id = lax.axis_index("dp").astype(I32)
    band_id = lax.axis_index("mp").astype(I32)
    samples, max_cams, _ = visible.shape
    slots, quarter, depth = images.shape
    channels = neck_weight.shape[1]
    queries = bev_query.shape[0]
    rows = slots * quarter
    flat_images = images.reshape(rows, depth)
    lanes, owner = call(
        pack_kernel,
        (
            jax.ShapeDtypeStruct((owners, quarter, 2 * channels), BF16),
            jax.ShapeDtypeStruct((8, slots), I32),
        ),
        owner_id[None],
        *(
            pltpu.with_memory_space_constraint(arg, pltpu.HBM)
            for arg in (
                cams.reshape(-1, min(128, cams.shape[0])),
                pack[None],
                flat_images,
                cam_keys.reshape(rows, channels),
                neck_weight,
            )
        ),
        specs=[smem()] + [pl.BlockSpec(memory_space=pltpu.HBM)] * 5,
        scratch=[
            pltpu.VMEM((cams.shape[0] // min(128, cams.shape[0]), min(128, cams.shape[0])), I32),
            pltpu.VMEM((1, pack.shape[0]), I32),
            pltpu.VMEM((rows, depth), BF16),
            pltpu.VMEM((rows, channels), BF16),
            pltpu.VMEM((depth, channels), BF16),
            pltpu.VMEM((rows, channels), BF16),
            pltpu.SMEM((8, slots), I32),
            pltpu.SemaphoreType.DMA((6,)),
        ],
        pinned=False,
    )
    got = lax.all_to_all(lanes, "dp", split_axis=0, concat_axis=0, tiled=True)
    cost = 1 << 30, 1 << 22
    chips = Y_CHIPS
    deep = owners // (CORES * chips)
    share = depth // (owners * bands)

    def device(y, z, c):
        return (y * deep + z) * CORES + c

    def place_of(device_id):
        return device_id // (deep * CORES), device_id // CORES % deep, device_id % CORES

    ys, zs, cs = range(chips), range(deep), range(CORES)
    my_y, _, my_core = place_of(owner_id)
    owner_y, owner_z, owner_core = place_of(owner[0])
    column = (owner_y - my_y) % chips * CORES + (owner_core + my_core) % CORES
    dealt = call(
        deal_kernel,
        jax.ShapeDtypeStruct((owners, quarter, depth), BF16),
        column * deep + owner_z,
        flat_images,
        specs=[smem(), vmem()],
        cost=cost,
    ).reshape(chips * CORES, deep, quarter, depth)
    pieces = [dealt[0]]
    for p in range(1, chips * CORES):
        moves = [
            (device(y, z, c), device((y + p // CORES) % chips, z, (c + p) % CORES))
            for y in ys
            for z in zs
            for c in cs
        ]
        pieces.append(lax.ppermute(dealt[p], "dp", moves))
    base, pull, gain = call(
        temporal_kernel,
        (
            pltpu.HBM((samples, queries, channels), F32),
            pltpu.HBM((samples, queries, channels), F32),
            on_chip((1, channels), F32),
        ),
        band_id[None],
        bev_query,
        point_weight,
        prev_bev,
        align,
        out_grad,
        norm_gain[None],
        specs=[smem()] + [vmem()] * 6,
        cost=cost,
    )
    first = owner_id * samples
    sample_ids = jnp.arange(cams.shape[0], dtype=I32)
    start = jnp.sum(jnp.where(sample_ids < first, cams, 0))
    local = lax.dynamic_slice(cams, (first,), (samples,))
    window = samples * max_cams
    padded = jnp.concatenate([pack, jnp.zeros((window,), I32)])
    bins = lax.dynamic_slice(padded, (start,), (window,)) // slots
    member = jnp.arange(samples, dtype=I32)
    offset = jnp.sum(jnp.where(member[None, :] < member[:, None], local[None, :], 0), axis=1)
    camera = jnp.arange(max_cams, dtype=I32)
    seen = (visible > 0).astype(I32)
    earlier = (camera[:, None] < camera[None, :]).astype(I32)
    rank = jnp.sum(seen[:, :, None, :] * earlier[None, :, :, None], axis=1)
    place = jnp.arange(SEEN, dtype=I32)
    chosen = (rank[:, :, :, None] == place) & (seen[:, :, :, None] > 0)
    position = jnp.sum(
        jnp.where(chosen, offset[:, None, None, None] + camera[None, :, None, None] + 1, 0), axis=1
    )
    in_window = position[..., None] == jnp.arange(1, window + 1, dtype=I32)
    lane_of = jnp.sum(jnp.where(in_window, bins + 1, 0), axis=-1) - 1
    lane_of = lane_of.transpose(1, 0, 2).reshape(bands * samples * SEEN)
    count = lax.dynamic_slice_in_dim(jnp.sum(seen, axis=1), band_id, 1, axis=1)[:, 0]
    source = jnp.maximum(lane_of, 0)
    bin_y, bin_z, bin_core = place_of(source)
    back_lane = (bin_z * chips + (my_y - bin_y) % chips) * CORES + (bin_core + my_core) % CORES
    got, base, pull, gain, pieces, source, back_lane, count = lax.optimization_barrier(
        (got, base, pull, gain, pieces, source, back_lane, count)
    )
    piece = samples * SEEN * quarter
    chosen_kv = call(
        select_kernel,
        on_chip((bands * samples * SEEN, quarter, 2 * channels), BF16),
        source,
        got,
        specs=[smem(), vmem()],
    )
    kv = lax.all_to_all(
        chosen_kv.reshape(bands, piece, 2 * channels), "mp", split_axis=0, concat_axis=0, tiled=True
    )
    tokens = owners * quarter
    turned = call(
        functools.partial(turn_kernel, bands=bands, share=share),
        pltpu.HBM((depth, tokens), BF16),
        *pieces,
        specs=[pl.BlockSpec(memory_space=pltpu.HBM)] * len(pieces),
        scratch=[
            pltpu.VMEM((deep, len(pieces), quarter, depth), BF16),
            pltpu.VMEM((tokens // 128, depth, 128), F32),
            pltpu.SemaphoreType.DMA((len(pieces),)),
        ],
        cost=cost,
    )
    kv, turned = lax.optimization_barrier((kv, turned))
    bev_out, grads = call(
        attention_kernel,
        (
            jax.ShapeDtypeStruct((samples, queries, channels), BF16),
            on_chip((bands, piece, channels), BF16),
        ),
        count,
        kv,
        base,
        pull,
        bev_query,
        gain,
        specs=[smem(), vmem()] + [pl.BlockSpec(memory_space=pltpu.HBM)] * 2 + [vmem()] * 2,
        scratch=[
            pltpu.VMEM((samples, queries, channels), F32),
            pltpu.VMEM((samples, queries, channels), F32),
            pltpu.SemaphoreType.DMA((2,)),
            pltpu.VMEM((HEADS * queries, channels), BF16),
            pltpu.VMEM((bands, piece, HEADS * queries), F32),
            pltpu.VMEM((samples, bands * SEEN * quarter, HEADS * queries), BF16),
            pltpu.VMEM((samples, queries, channels), F32),
            pltpu.VMEM((samples, queries, channels), BF16),
        ],
    )
    grads = lax.all_to_all(grads, "mp", split_axis=0, concat_axis=0, tiled=True)
    back = call(
        return_kernel,
        on_chip((owners, quarter, channels), BF16),
        back_lane,
        grads.reshape(bands * samples * SEEN, quarter, channels),
        specs=[smem(), vmem()],
        scratch=[pltpu.VMEM((owners, quarter, channels), F32)],
    )

    def exchange(part, axis, groups):
        return lax.all_to_all(
            part, axis, split_axis=0, concat_axis=0, tiled=True, axis_index_groups=groups
        )

    columns = [[device(y, z, c) for z in zs] for y in ys for c in cs]
    back = exchange(back.reshape(deep, tokens // deep, channels), "dp", columns)
    neck = call(
        functools.partial(neck_kernel, samples=cams.shape[0]),
        on_chip((depth, channels), BF16),
        back.reshape(tokens, channels),
        turned,
    )
    planes = [
        [device(y, z, c) * bands + x for y in ys for c in cs for x in range(bands)] for z in zs
    ]
    neck = neck.reshape(chips * CORES * bands, share * deep, channels)
    neck = exchange(neck, ("dp", "mp"), planes).astype(F32)
    neck = jnp.sum(neck, axis=0).reshape(share, deep, channels).transpose(1, 0, 2)
    neck = exchange(neck, "dp", columns)
    return bev_out, jnp.sum(neck, axis=0)


def solution(mesh):
    return jax.shard_map(
        on_device,
        mesh=mesh,
        in_specs=(
            P(),
            P(),
            P("dp", None, None),
            P("dp", None, "mp"),
            P("dp", "mp", None),
            P("dp", "mp", None),
            P(),
            P("mp", None),
            P("dp", "mp", None),
            P(),
            P(),
            P("dp", "mp", None),
        ),
        out_specs=(P("dp", "mp", None), P(("dp", "mp"), None)),
        check_vma=False,
    )
```

```python
import functools

import jax
import jax.numpy as jnp
from jax import lax
from jax.experimental import pallas as pl
from jax.experimental.pallas import tpu as pltpu
from jax.sharding import PartitionSpec as P

HEADS = 8
KT = 4
CORES = 2
Y_CHIPS = 4
SEEN = 3

NORM_EPS = 1e-05
MASKED = -1e30
LOG2_E = 1.4426950408889634
BF16 = jnp.bfloat16
F32 = jnp.float32
I32 = jnp.int32


def dot(a, b, a_dim=1, b_dim=0):
    return lax.dot_general(a, b, (((a_dim,), (b_dim,)), ((), ())), preferred_element_type=F32)


def iota(shape, dim):
    return lax.broadcasted_iota(I32, shape, dim)


def vmem():
    return pl.BlockSpec(memory_space=pltpu.VMEM)


def smem():
    return pl.BlockSpec(memory_space=pltpu.SMEM)


def on_chip(shape, dtype):
    return pltpu.VMEM(shape, dtype)


def call(body, outs, *args, specs=None, scratch=(), cost=(1 << 20, 1 << 20), pinned=True):
    specs = specs or [vmem()] * len(args)
    if pinned:
        args = [
            pltpu.with_memory_space_constraint(arg, spec.memory_space) for arg, spec in zip(args, specs)
        ]
    return pl.pallas_call(
        body,
        out_shape=outs,
        in_specs=specs,
        out_specs=jax.tree.map(lambda _: vmem(), outs),
        scratch_shapes=scratch,
        compiler_params=pltpu.CompilerParams(vmem_limit_bytes=24 << 20),
        cost_estimate=pl.CostEstimate(flops=cost[0], bytes_accessed=cost[1], transcendentals=0),
    )(*args)


def pack_kernel(
    bin_ref,
    cams_hbm,
    pack_hbm,
    image_hbm,
    key_hbm,
    weight_hbm,
    lane_ref,
    owner_ref,
    cams_ref,
    pack_ref,
    image_ref,
    key_ref,
    weight_ref,
    feature_ref,
    index_ref,
    sems,
    *,
    pack_slots,
):
    moves = [
        pltpu.make_async_copy(source, target, sems.at[i])
        for i, (source, target) in enumerate(
            (
                (cams_hbm, cams_ref),
                (pack_hbm, pack_ref),
                (image_hbm, image_ref),
                (weight_hbm, weight_ref),
                (key_hbm, key_ref),
            )
        )
    ]
    for move in moves:
        move.start()
    cameras = pack_ref.shape[1]
    rows, channels = key_ref.shape
    slots = pack_slots
    owners, quarter, _ = lane_ref.shape
    groups, width = cams_ref.shape
    spd = groups * width // owners
    lane_ref[...] = jnp.zeros(lane_ref.shape, BF16)
    moves[0].wait()
    first = iota((owners, width), 0) * spd
    before = jnp.zeros((owners, width), F32)
    for g in range(groups):
        counts = cams_ref[g : g + 1, :].astype(F32)
        before += jnp.where(iota((owners, width), 1) + g * width < first, counts, 0.0)
    start = jnp.sum(before, axis=1, keepdims=True)
    start = jnp.sum(
        jnp.where(iota((owners, owners), 0) == iota((owners, owners), 1), start, 0.0), axis=0, keepdims=True
    )
    moves[1].wait()
    here = (pack_ref[...] - bin_ref[0] * slots) == iota((slots, cameras), 0)
    number = iota((1, cameras), 1).astype(F32)
    camera = jnp.sum(jnp.where(here, number, 0.0), axis=1, keepdims=True)
    owner = jnp.sum((start <= camera).astype(F32), axis=1, keepdims=True) - 1.0
    across = (slots, owner_ref.shape[1])
    owner = jnp.sum(jnp.where(iota(across, 0) == iota(across, 1), owner, 0.0), axis=0, keepdims=True)
    owner_ref[...] = jnp.broadcast_to(owner, owner_ref.shape).astype(I32)
    index = pltpu.make_async_copy(owner_ref, index_ref, sems.at[5])
    index.start()
    moves[2].wait()
    moves[3].wait()
    feature_ref[...] = dot(image_ref[...], weight_ref[...]).astype(BF16)
    index.wait()
    moves[4].wait()
    for s in range(slots):
        here = slice(s * quarter, (s + 1) * quarter)
        lane_ref[index_ref[0, s], :, :channels] = feature_ref[here, :]
        lane_ref[index_ref[0, s], :, channels:] = key_ref[here, :]


def deal_kernel(lane_ref, image_ref, out_ref):
    quarter = out_ref.shape[1]
    out_ref[...] = jnp.zeros(out_ref.shape, BF16)
    for s in range(image_ref.shape[0] // quarter):
        out_ref[lane_ref[s]] = image_ref[s * quarter : (s + 1) * quarter, :]


def turn_kernel(*refs, bands, share):
    out_ref, block_ref, turned_ref, sems = refs[-4:]
    pieces = refs[:-4]
    deep, quarter, _ = pieces[0].shape
    moves = [
        pltpu.make_async_copy(piece, block_ref.at[:, p], sems.at[p]) for p, piece in enumerate(pieces)
    ]
    for move in moves:
        move.start()
    for move in moves:
        move.wait()
    groups, depth, width = turned_ref.shape
    some = width // (len(pieces) * quarter)
    for g in range(groups):
        block = block_ref[g * some : (g + 1) * some].reshape(width, depth)
        turned_ref[g] = block.astype(F32).T
    step = CORES * bands * share
    at = 0
    for y in range(len(pieces) // CORES):
        for c in range(CORES):
            for j in range(bands * share):
                first = y * deep * step + c * bands * share + j
                for g in range(groups):
                    part = turned_ref.at[g][pl.ds(first, deep, stride=step), :]
                    out_ref[at : at + deep, g * width : (g + 1) * width] = part.astype(BF16)
                at += deep


def temporal_kernel(
    band_ref,
    query_ref,
    point_ref,
    prev_ref,
    align_ref,
    cotangent_ref,
    gain_ref,
    base_ref,
    pull_ref,
    scale_ref,
):
    samples, cells, channels = prev_ref.shape
    query = query_ref[...]
    head_dim = channels // HEADS
    wide = query.astype(F32)
    gain = gain_ref[...]
    scale_ref[...] = gain
    gates = []
    for k in range(KT):
        shape = (HEADS * KT, channels)
        pick = iota(shape, 0) == (iota(shape, 1) // head_dim) * KT + k
        weight = dot(point_ref[...], pick.astype(F32).astype(BF16)).astype(BF16)
        gates.append(jax.nn.sigmoid(dot(query, weight)))
    for m in range(samples):
        total = wide
        for k in range(KT):
            cell = align_ref[m, k : k + 1, :] - band_ref[0] * cells
            pick = (iota((cells, cells), 0) == cell).astype(F32).astype(BF16)
            total = total + gates[k] * dot(pick, prev_ref[m], 0, 0)
        base_ref[m] = total
        pull = cotangent_ref[m].astype(F32) * gain
        pull_ref[m] = pull - jnp.mean(pull, axis=1, keepdims=True)


def select_kernel(source_ref, lane_ref, out_ref):
    for e in range(out_ref.shape[0]):
        out_ref[e] = lane_ref[source_ref[e]]


def attention_kernel(
    count_ref,
    kv_ref,
    base_hbm,
    pull_hbm,
    query_ref,
    gain_ref,
    out_ref,
    grad_ref,
    base_ref,
    pull_ref,
    sems,
    heads_ref,
    score_ref,
    prob_ref,
    norm_ref,
    cross_ref,
):
    moves = [
        pltpu.make_async_copy(base_hbm, base_ref, sems.at[0]),
        pltpu.make_async_copy(pull_hbm, pull_ref, sems.at[1]),
    ]
    for move in moves:
        move.start()
    parts, rows, width = kv_ref.shape
    samples, queries, channels = base_ref.shape
    step = rows // samples
    keys = parts * step
    head_dim = channels // HEADS
    quarter = step // SEEN
    gain = gain_ref[...]
    lane_head = iota((1, channels), 1) // head_dim
    masks = [(lane_head == h).astype(F32).astype(BF16) for h in range(HEADS)]
    factor = float(head_dim) ** -0.5 * LOG2_E
    place = iota((keys, HEADS * queries), 0) % step // quarter
    for h in range(HEADS):
        heads_ref[h * queries : (h + 1) * queries, :] = query_ref[...] * masks[h]
    spans = [slice(m * step, (m + 1) * step) for m in range(samples)]
    ray = kv_ref[:, :, channels:].reshape(parts * rows, channels)
    score_ref[...] = dot(ray, heads_ref[...], 1, 1).reshape(score_ref.shape)
    for m in range(samples):
        scores = score_ref[:, spans[m], :].reshape(keys, HEADS * queries)
        scores = jnp.where(place < count_ref[m], scores, MASKED)
        raised = jnp.exp2((scores - jnp.max(scores, axis=0, keepdims=True)) * factor)
        prob_ref[m] = (raised * (1.0 / jnp.sum(raised, axis=0, keepdims=True))).astype(BF16)
    moves[0].wait()
    for m in range(samples):
        values = kv_ref[:, spans[m], :channels].reshape(keys, channels)
        values = jnp.concatenate([values * mask for mask in masks], axis=0)
        probs = prob_ref[m]
        tall = jnp.concatenate(
            [probs[:, h * queries : (h + 1) * queries] for h in range(HEADS)], axis=0
        )
        norm_ref[m] = base_ref[m] + dot(tall, values, 0, 0)
    moves[1].wait()
    for m in range(samples):
        pre_norm = norm_ref[m]
        centred = pre_norm - jnp.mean(pre_norm, axis=1, keepdims=True)
        scale = lax.rsqrt(jnp.mean(centred * centred, axis=1, keepdims=True) + NORM_EPS)
        unit = centred * scale
        out_ref[m] = (unit * gain).astype(BF16)
        pull = pull_ref[m]
        pull = pull - unit * jnp.mean(pull * unit, axis=1, keepdims=True)
        cross_ref[m] = (pull * scale).astype(BF16)
    for m in range(samples):
        pull = cross_ref[m]
        pull = jnp.concatenate([pull * mask for mask in masks], axis=0)
        grad_ref[:, spans[m], :] = dot(prob_ref[m], pull).astype(BF16).reshape(parts, step, channels)


def return_kernel(source_ref, grad_ref, lane_ref, sum_ref):
    sum_ref[...] = jnp.zeros(sum_ref.shape, F32)
    for e in range(grad_ref.shape[0]):
        lane = source_ref[e]
        sum_ref[lane] = sum_ref[lane] + grad_ref[e].astype(F32)
    lane_ref[...] = sum_ref[...].astype(BF16)


def neck_kernel(grad_ref, turned_ref, out_ref, *, samples):
    out_ref[...] = (dot(turned_ref[...], grad_ref[...]) * (1.0 / samples)).astype(BF16)


def on_device(
    cams,
    pack,
    visible,
    align,
    images,
    cam_keys,
    neck_weight,
    bev_query,
    prev_bev,
    point_weight,
    norm_gain,
    out_grad,
):
    owners = lax.axis_size("dp")
    bands = lax.axis_size("mp")
    owner_id = lax.axis_index("dp").astype(I32)
    band_id = lax.axis_index("mp").astype(I32)
    samples, max_cams, _ = visible.shape
    slots, quarter, depth = images.shape
    channels = neck_weight.shape[1]
    queries = bev_query.shape[0]
    rows = slots * quarter
    flat_images = images.reshape(rows, depth)
    lanes, owner = call(
        functools.partial(pack_kernel, pack_slots=slots),
        (
            jax.ShapeDtypeStruct((owners, quarter, 2 * channels), BF16),
            jax.ShapeDtypeStruct((8, 128), I32),
        ),
        owner_id[None],
        *(
            pltpu.with_memory_space_constraint(arg, pltpu.HBM)
            for arg in (
                cams.reshape(-1, min(128, cams.shape[0])),
                pack[None],
                flat_images,
                cam_keys.reshape(rows, channels),
                neck_weight,
            )
        ),
        specs=[smem()] + [pl.BlockSpec(memory_space=pltpu.HBM)] * 5,
        scratch=[
            pltpu.VMEM((cams.shape[0] // min(128, cams.shape[0]), min(128, cams.shape[0])), I32),
            pltpu.VMEM((1, pack.shape[0]), I32),
            pltpu.VMEM((rows, depth), BF16),
            pltpu.VMEM((rows, channels), BF16),
            pltpu.VMEM((depth, channels), BF16),
            pltpu.VMEM((rows, channels), BF16),
            pltpu.SMEM((8, 128), I32),
            pltpu.SemaphoreType.DMA((6,)),
        ],
        pinned=False,
    )
    got = lax.all_to_all(lanes, "dp", split_axis=0, concat_axis=0, tiled=True)
    cost = 1 << 30, 1 << 22
    chips = Y_CHIPS
    deep = owners // (CORES * chips)
    share = depth // (owners * bands)

    def device(y, z, c):
        return (y * deep + z) * CORES + c

    def place_of(device_id):
        return device_id // (deep * CORES), device_id // CORES % deep, device_id % CORES

    ys, zs, cs = range(chips), range(deep), range(CORES)
    my_y, _, my_core = place_of(owner_id)
    owner_y, owner_z, owner_core = place_of(owner[0, :slots])
    column = (owner_y - my_y) % chips * CORES + (owner_core + my_core) % CORES
    dealt = call(
        deal_kernel,
        jax.ShapeDtypeStruct((owners, quarter, depth), BF16),
        column * deep + owner_z,
        flat_images,
        specs=[smem(), vmem()],
        cost=cost,
    ).reshape(chips * CORES, deep, quarter, depth)
    pieces = [dealt[0]]
    for p in range(1, chips * CORES):
        moves = [
            (device(y, z, c), device((y + p // CORES) % chips, z, (c + p) % CORES))
            for y in ys
            for z in zs
            for c in cs
        ]
        pieces.append(lax.ppermute(dealt[p], "dp", moves))
    base, pull, gain = call(
        temporal_kernel,
        (
            pltpu.HBM((samples, queries, channels), F32),
            pltpu.HBM((samples, queries, channels), F32),
            on_chip((1, channels), F32),
        ),
        band_id[None],
        bev_query,
        point_weight,
        prev_bev,
        align,
        out_grad,
        norm_gain[None],
        specs=[smem()] + [vmem()] * 6,
        cost=cost,
    )
    first = owner_id * samples
    sample_ids = jnp.arange(cams.shape[0], dtype=I32)
    start = jnp.sum(jnp.where(sample_ids < first, cams, 0))
    local = lax.dynamic_slice(cams, (first,), (samples,))
    window = samples * max_cams
    padded = jnp.concatenate([pack, jnp.zeros((window,), I32)])
    bins = lax.dynamic_slice(padded, (start,), (window,)) // slots
    member = jnp.arange(samples, dtype=I32)
    offset = jnp.sum(jnp.where(member[None, :] < member[:, None], local[None, :], 0), axis=1)
    camera = jnp.arange(max_cams, dtype=I32)
    seen = (visible > 0).astype(I32)
    earlier = (camera[:, None] < camera[None, :]).astype(I32)
    rank = jnp.sum(seen[:, :, None, :] * earlier[None, :, :, None], axis=1)
    place = jnp.arange(SEEN, dtype=I32)
    chosen = (rank[:, :, :, None] == place) & (seen[:, :, :, None] > 0)
    position = jnp.sum(
        jnp.where(chosen, offset[:, None, None, None] + camera[None, :, None, None] + 1, 0), axis=1
    )
    in_window = position[..., None] == jnp.arange(1, window + 1, dtype=I32)
    lane_of = jnp.sum(jnp.where(in_window, bins + 1, 0), axis=-1) - 1
    lane_of = lane_of.transpose(1, 0, 2).reshape(bands * samples * SEEN)
    count = lax.dynamic_slice_in_dim(jnp.sum(seen, axis=1), band_id, 1, axis=1)[:, 0]
    source = jnp.maximum(lane_of, 0)
    bin_y, bin_z, bin_core = place_of(source)
    back_lane = (bin_z * chips + (my_y - bin_y) % chips) * CORES + (bin_core + my_core) % CORES
    got, base, pull, gain, pieces, source, back_lane, count = lax.optimization_barrier(
        (got, base, pull, gain, pieces, source, back_lane, count)
    )
    piece = samples * SEEN * quarter
    chosen_kv = call(
        select_kernel,
        on_chip((bands * samples * SEEN, quarter, 2 * channels), BF16),
        source,
        got,
        specs=[smem(), vmem()],
    )
    kv = lax.all_to_all(
        chosen_kv.reshape(bands, piece, 2 * channels), "mp", split_axis=0, concat_axis=0, tiled=True
    )
    bev_out, grads = call(
        attention_kernel,
        (
            jax.ShapeDtypeStruct((samples, queries, channels), BF16),
            on_chip((bands, piece, channels), BF16),
        ),
        count,
        kv,
        base,
        pull,
        bev_query,
        gain,
        specs=[smem(), vmem()] + [pl.BlockSpec(memory_space=pltpu.HBM)] * 2 + [vmem()] * 2,
        scratch=[
            pltpu.VMEM((samples, queries, channels), F32),
            pltpu.VMEM((samples, queries, channels), F32),
            pltpu.SemaphoreType.DMA((2,)),
            pltpu.VMEM((HEADS * queries, channels), BF16),
            pltpu.VMEM((bands, piece, HEADS * queries), F32),
            pltpu.VMEM((samples, bands * SEEN * quarter, HEADS * queries), BF16),
            pltpu.VMEM((samples, queries, channels), F32),
            pltpu.VMEM((samples, queries, channels), BF16),
        ],
    )
    grads = lax.all_to_all(grads, "mp", split_axis=0, concat_axis=0, tiled=True)
    grads, pieces = lax.optimization_barrier((grads, pieces))
    back = call(
        return_kernel,
        on_chip((owners, quarter, channels), BF16),
        back_lane,
        grads.reshape(bands * samples * SEEN, quarter, channels),
        specs=[smem(), vmem()],
        scratch=[pltpu.VMEM((owners, quarter, channels), F32)],
    )

    def exchange(part, axis, groups):
        return lax.all_to_all(
            part, axis, split_axis=0, concat_axis=0, tiled=True, axis_index_groups=groups
        )

    columns = [[device(y, z, c) for z in zs] for y in ys for c in cs]
    tokens = owners * quarter
    turned = call(
        functools.partial(turn_kernel, bands=bands, share=share),
        on_chip((depth, tokens), BF16),
        *pieces,
        specs=[pl.BlockSpec(memory_space=pltpu.HBM)] * len(pieces),
        scratch=[
            pltpu.VMEM((deep, len(pieces), quarter, depth), BF16),
            pltpu.VMEM((tokens // 128, depth, 128), F32),
            pltpu.SemaphoreType.DMA((len(pieces),)),
        ],
        cost=cost,
    )
    back = exchange(back.reshape(deep, tokens // deep, channels), "dp", columns)
    neck = call(
        functools.partial(neck_kernel, samples=cams.shape[0]),
        on_chip((depth, channels), BF16),
        back.reshape(tokens, channels),
        turned,
    )
    planes = [
        [device(y, z, c) * bands + x for y in ys for c in cs for x in range(bands)] for z in zs
    ]
    neck = neck.reshape(chips * CORES * bands, share * deep, channels)
    neck = exchange(neck, ("dp", "mp"), planes).astype(F32)
    neck = jnp.sum(neck, axis=0).reshape(share, deep, channels).transpose(1, 0, 2)
    neck = exchange(neck, "dp", columns)
    return bev_out, jnp.sum(neck, axis=0)


def solution(mesh):
    return jax.shard_map(
        on_device,
        mesh=mesh,
        in_specs=(
            P(),
            P(),
            P("dp", None, None),
            P("dp", None, "mp"),
            P("dp", "mp", None),
            P("dp", "mp", None),
            P(),
            P("mp", None),
            P("dp", "mp", None),
            P(),
            P(),
            P("dp", "mp", None),
        ),
        out_specs=(P("dp", "mp", None), P(("dp", "mp"), None)),
        check_vma=False,
    )
```

```python
import functools

import jax
import jax.numpy as jnp
from jax import lax
from jax.experimental import pallas as pl
from jax.experimental.pallas import tpu as pltpu
from jax.sharding import PartitionSpec as P

HEADS = 8
KT = 4
CORES = 2
Y_CHIPS = 4
SEEN = 3

NORM_EPS = 1e-05
MASKED = -1e30
LOG2_E = 1.4426950408889634
BF16 = jnp.bfloat16
F32 = jnp.float32
I32 = jnp.int32


def dot(a, b, a_dim=1, b_dim=0):
    return lax.dot_general(a, b, (((a_dim,), (b_dim,)), ((), ())), preferred_element_type=F32)


def iota(shape, dim):
    return lax.broadcasted_iota(I32, shape, dim)


def vmem():
    return pl.BlockSpec(memory_space=pltpu.VMEM)


def smem():
    return pl.BlockSpec(memory_space=pltpu.SMEM)


def on_chip(shape, dtype):
    return pltpu.VMEM(shape, dtype)


def call(body, outs, *args, specs=None, scratch=(), cost=(1 << 20, 1 << 20), pinned=True):
    specs = specs or [vmem()] * len(args)
    if pinned:
        args = [
            pltpu.with_memory_space_constraint(arg, spec.memory_space) for arg, spec in zip(args, specs)
        ]
    return pl.pallas_call(
        body,
        out_shape=outs,
        in_specs=specs,
        out_specs=jax.tree.map(lambda _: vmem(), outs),
        scratch_shapes=scratch,
        compiler_params=pltpu.CompilerParams(vmem_limit_bytes=24 << 20),
        cost_estimate=pl.CostEstimate(flops=cost[0], bytes_accessed=cost[1], transcendentals=0),
    )(*args)


def pack_kernel(
    bin_ref,
    cams_hbm,
    pack_hbm,
    image_hbm,
    key_hbm,
    weight_hbm,
    lane_ref,
    owner_ref,
    cams_ref,
    pack_ref,
    image_ref,
    key_ref,
    weight_ref,
    feature_ref,
    index_ref,
    sems,
    *,
    pack_slots,
):
    moves = [
        pltpu.make_async_copy(source, target, sems.at[i])
        for i, (source, target) in enumerate(
            (
                (cams_hbm, cams_ref),
                (pack_hbm, pack_ref),
                (image_hbm, image_ref),
                (weight_hbm, weight_ref),
                (key_hbm, key_ref),
            )
        )
    ]
    for move in moves:
        move.start()
    cameras = pack_ref.shape[1]
    rows, channels = key_ref.shape
    slots = pack_slots
    owners, quarter, _ = lane_ref.shape
    groups, width = cams_ref.shape
    spd = groups * width // owners
    moves[0].wait()
    first = iota((owners, width), 0) * spd
    before = jnp.zeros((owners, width), F32)
    for g in range(groups):
        counts = cams_ref[g : g + 1, :].astype(F32)
        before += jnp.where(iota((owners, width), 1) + g * width < first, counts, 0.0)
    start = jnp.sum(before, axis=1, keepdims=True)
    start = jnp.sum(
        jnp.where(iota((owners, owners), 0) == iota((owners, owners), 1), start, 0.0), axis=0, keepdims=True
    )
    moves[1].wait()
    here = (pack_ref[...] - bin_ref[0] * slots) == iota((slots, cameras), 0)
    number = iota((1, cameras), 1).astype(F32)
    camera = jnp.sum(jnp.where(here, number, 0.0), axis=1, keepdims=True)
    owner = jnp.sum((start <= camera).astype(F32), axis=1, keepdims=True) - 1.0
    across = (slots, owner_ref.shape[1])
    owner = jnp.sum(jnp.where(iota(across, 0) == iota(across, 1), owner, 0.0), axis=0, keepdims=True)
    owner_ref[...] = jnp.broadcast_to(owner, owner_ref.shape).astype(I32)
    index = pltpu.make_async_copy(owner_ref, index_ref, sems.at[5])
    index.start()
    moves[2].wait()
    moves[3].wait()
    feature_ref[...] = dot(image_ref[...], weight_ref[...]).astype(BF16)
    index.wait()
    moves[4].wait()
    for s in range(slots):
        here = slice(s * quarter, (s + 1) * quarter)
        lane_ref[index_ref[0, s], :, :channels] = feature_ref[here, :]
        lane_ref[index_ref[0, s], :, channels:] = key_ref[here, :]


def deal_kernel(lane_ref, image_ref, out_ref):
    quarter = out_ref.shape[1]
    out_ref[...] = jnp.zeros(out_ref.shape, BF16)
    for s in range(image_ref.shape[0] // quarter):
        out_ref[lane_ref[s]] = image_ref[s * quarter : (s + 1) * quarter, :]


def turn_kernel(*refs, bands, share):
    out_ref, block_ref, turned_ref, sems = refs[-4:]
    pieces = refs[:-4]
    deep, quarter, _ = pieces[0].shape
    moves = [
        pltpu.make_async_copy(piece, block_ref.at[:, p], sems.at[p]) for p, piece in enumerate(pieces)
    ]
    for move in moves:
        move.start()
    for move in moves:
        move.wait()
    groups, depth, width = turned_ref.shape
    some = width // (len(pieces) * quarter)
    for g in range(groups):
        block = block_ref[g * some : (g + 1) * some].reshape(width, depth)
        turned_ref[g] = block.astype(F32).T
    step = CORES * bands * share
    at = 0
    for y in range(len(pieces) // CORES):
        for c in range(CORES):
            for j in range(bands * share):
                first = y * deep * step + c * bands * share + j
                for g in range(groups):
                    part = turned_ref.at[g][pl.ds(first, deep, stride=step), :]
                    out_ref[at : at + deep, g * width : (g + 1) * width] = part.astype(BF16)
                at += deep


def temporal_kernel(
    band_ref,
    query_ref,
    point_ref,
    prev_ref,
    align_ref,
    cotangent_ref,
    gain_ref,
    base_ref,
    pull_ref,
    heads_ref,
    scale_ref,
):
    samples, cells, channels = prev_ref.shape
    query = query_ref[...]
    head_dim = channels // HEADS
    wide = query.astype(F32)
    gain = gain_ref[...]
    scale_ref[...] = gain
    for h in range(HEADS):
        mask = (iota((1, channels), 1) // head_dim == h).astype(F32).astype(BF16)
        heads_ref[h * cells : (h + 1) * cells, :] = query * mask
    gates = []
    for k in range(KT):
        shape = (HEADS * KT, channels)
        pick = iota(shape, 0) == (iota(shape, 1) // head_dim) * KT + k
        weight = dot(point_ref[...], pick.astype(F32).astype(BF16)).astype(BF16)
        gates.append(jax.nn.sigmoid(dot(query, weight)))
    for m in range(samples):
        total = wide
        for k in range(KT):
            cell = align_ref[m, k : k + 1, :] - band_ref[0] * cells
            pick = (iota((cells, cells), 0) == cell).astype(F32).astype(BF16)
            total = total + gates[k] * dot(pick, prev_ref[m], 0, 0)
        base_ref[m] = total
        pull = cotangent_ref[m].astype(F32) * gain
        pull_ref[m] = pull - jnp.mean(pull, axis=1, keepdims=True)


def select_kernel(source_ref, lane_ref, out_ref):
    for e in range(out_ref.shape[0]):
        out_ref[e] = lane_ref[source_ref[e]]


def attention_kernel(
    count_ref,
    kv_ref,
    base_ref,
    pull_hbm,
    heads_ref,
    gain_ref,
    out_ref,
    grad_ref,
    pull_ref,
    sem,
    score_ref,
    prob_ref,
    norm_ref,
    cross_ref,
):
    move = pltpu.make_async_copy(pull_hbm, pull_ref, sem)
    move.start()
    parts, rows, width = kv_ref.shape
    samples, queries, channels = base_ref.shape
    step = rows // samples
    keys = parts * step
    head_dim = channels // HEADS
    quarter = step // SEEN
    gain = gain_ref[...]
    lane_head = iota((1, channels), 1) // head_dim
    masks = [(lane_head == h).astype(F32).astype(BF16) for h in range(HEADS)]
    factor = float(head_dim) ** -0.5 * LOG2_E
    place = iota((keys, HEADS * queries), 0) % step // quarter
    spans = [slice(m * step, (m + 1) * step) for m in range(samples)]
    ray = kv_ref[:, :, channels:].reshape(parts * rows, channels)
    score_ref[...] = dot(ray, heads_ref[...], 1, 1).reshape(score_ref.shape)
    for m in range(samples):
        scores = score_ref[:, spans[m], :].reshape(keys, HEADS * queries)
        scores = jnp.where(place < count_ref[m], scores, MASKED)
        raised = jnp.exp2((scores - jnp.max(scores, axis=0, keepdims=True)) * factor)
        prob_ref[m] = (raised * (1.0 / jnp.sum(raised, axis=0, keepdims=True))).astype(BF16)
    for m in range(samples):
        values = kv_ref[:, spans[m], :channels].reshape(keys, channels)
        values = jnp.concatenate([values * mask for mask in masks], axis=0)
        probs = prob_ref[m]
        tall = jnp.concatenate(
            [probs[:, h * queries : (h + 1) * queries] for h in range(HEADS)], axis=0
        )
        norm_ref[m] = base_ref[m] + dot(tall, values, 0, 0)
    move.wait()
    for m in range(samples):
        pre_norm = norm_ref[m]
        centred = pre_norm - jnp.mean(pre_norm, axis=1, keepdims=True)
        scale = lax.rsqrt(jnp.mean(centred * centred, axis=1, keepdims=True) + NORM_EPS)
        unit = centred * scale
        out_ref[m] = (unit * gain).astype(BF16)
        pull = pull_ref[m]
        pull = pull - unit * jnp.mean(pull * unit, axis=1, keepdims=True)
        cross_ref[m] = (pull * scale).astype(BF16)
    for m in range(samples):
        pull = cross_ref[m]
        pull = jnp.concatenate([pull * mask for mask in masks], axis=0)
        grad_ref[:, spans[m], :] = dot(prob_ref[m], pull).astype(BF16).reshape(parts, step, channels)


def return_kernel(source_ref, grad_ref, lane_ref, sum_ref):
    sum_ref[...] = jnp.zeros(sum_ref.shape, F32)
    for e in range(grad_ref.shape[0]):
        lane = source_ref[e]
        sum_ref[lane] = sum_ref[lane] + grad_ref[e].astype(F32)
    lane_ref[...] = sum_ref[...].astype(BF16)


def neck_kernel(grad_ref, turned_ref, out_ref, *, samples):
    out_ref[...] = (dot(turned_ref[...], grad_ref[...]) * (1.0 / samples)).astype(BF16)


def on_device(
    cams,
    pack,
    visible,
    align,
    images,
    cam_keys,
    neck_weight,
    bev_query,
    prev_bev,
    point_weight,
    norm_gain,
    out_grad,
):
    owners = lax.axis_size("dp")
    bands = lax.axis_size("mp")
    owner_id = lax.axis_index("dp").astype(I32)
    band_id = lax.axis_index("mp").astype(I32)
    samples, max_cams, _ = visible.shape
    slots, quarter, depth = images.shape
    channels = neck_weight.shape[1]
    queries = bev_query.shape[0]
    rows = slots * quarter
    flat_images = images.reshape(rows, depth)
    lanes, owner = call(
        functools.partial(pack_kernel, pack_slots=slots),
        (
            jax.ShapeDtypeStruct((owners, quarter, 2 * channels), BF16),
            jax.ShapeDtypeStruct((8, 128), I32),
        ),
        owner_id[None],
        *(
            pltpu.with_memory_space_constraint(arg, pltpu.HBM)
            for arg in (
                cams.reshape(-1, min(128, cams.shape[0])),
                pack[None],
                flat_images,
                cam_keys.reshape(rows, channels),
                neck_weight,
            )
        ),
        specs=[smem()] + [pl.BlockSpec(memory_space=pltpu.HBM)] * 5,
        scratch=[
            pltpu.VMEM((cams.shape[0] // min(128, cams.shape[0]), min(128, cams.shape[0])), I32),
            pltpu.VMEM((1, pack.shape[0]), I32),
            pltpu.VMEM((rows, depth), BF16),
            pltpu.VMEM((rows, channels), BF16),
            pltpu.VMEM((depth, channels), BF16),
            pltpu.VMEM((rows, channels), BF16),
            pltpu.SMEM((8, 128), I32),
            pltpu.SemaphoreType.DMA((6,)),
        ],
        pinned=False,
    )
    got = lax.all_to_all(lanes, "dp", split_axis=0, concat_axis=0, tiled=True)
    cost = 1 << 30, 1 << 22
    chips = Y_CHIPS
    deep = owners // (CORES * chips)
    share = depth // (owners * bands)

    def device(y, z, c):
        return (y * deep + z) * CORES + c

    def place_of(device_id):
        return device_id // (deep * CORES), device_id // CORES % deep, device_id % CORES

    ys, zs, cs = range(chips), range(deep), range(CORES)
    my_y, _, my_core = place_of(owner_id)
    owner_y, owner_z, owner_core = place_of(owner[0, :slots])
    column = (owner_y - my_y) % chips * CORES + (owner_core + my_core) % CORES
    dealt = call(
        deal_kernel,
        jax.ShapeDtypeStruct((owners, quarter, depth), BF16),
        column * deep + owner_z,
        flat_images,
        specs=[smem(), vmem()],
        cost=cost,
    ).reshape(chips * CORES, deep, quarter, depth)
    pieces = [dealt[0]]
    for p in range(1, chips * CORES):
        moves = [
            (device(y, z, c), device((y + p // CORES) % chips, z, (c + p) % CORES))
            for y in ys
            for z in zs
            for c in cs
        ]
        pieces.append(lax.ppermute(dealt[p], "dp", moves))
    base, pull, heads, gain = call(
        temporal_kernel,
        (
            on_chip((samples, queries, channels), F32),
            pltpu.HBM((samples, queries, channels), F32),
            on_chip((HEADS * queries, channels), BF16),
            on_chip((1, channels), F32),
        ),
        band_id[None],
        bev_query,
        point_weight,
        prev_bev,
        align,
        out_grad,
        norm_gain[None],
        specs=[smem()] + [vmem()] * 6,
        cost=cost,
    )
    first = owner_id * samples
    sample_ids = jnp.arange(cams.shape[0], dtype=I32)
    start = jnp.sum(jnp.where(sample_ids < first, cams, 0))
    local = lax.dynamic_slice(cams, (first,), (samples,))
    window = samples * max_cams
    padded = jnp.concatenate([pack, jnp.zeros((window,), I32)])
    bins = lax.dynamic_slice(padded, (start,), (window,)) // slots
    member = jnp.arange(samples, dtype=I32)
    offset = jnp.sum(jnp.where(member[None, :] < member[:, None], local[None, :], 0), axis=1)
    camera = jnp.arange(max_cams, dtype=I32)
    seen = (visible > 0).astype(I32)
    earlier = (camera[:, None] < camera[None, :]).astype(I32)
    rank = jnp.sum(seen[:, :, None, :] * earlier[None, :, :, None], axis=1)
    place = jnp.arange(SEEN, dtype=I32)
    chosen = (rank[:, :, :, None] == place) & (seen[:, :, :, None] > 0)
    position = jnp.sum(
        jnp.where(chosen, offset[:, None, None, None] + camera[None, :, None, None] + 1, 0), axis=1
    )
    in_window = position[..., None] == jnp.arange(1, window + 1, dtype=I32)
    lane_of = jnp.sum(jnp.where(in_window, bins + 1, 0), axis=-1) - 1
    lane_of = jnp.where(lane_of >= 0, lane_of, lane_of[:, :, :1])
    lane_of = lane_of.transpose(1, 0, 2).reshape(bands * samples * SEEN)
    count = lax.dynamic_slice_in_dim(jnp.sum(seen, axis=1), band_id, 1, axis=1)[:, 0]
    source = jnp.maximum(lane_of, 0)
    bin_y, bin_z, bin_core = place_of(source)
    back_lane = (bin_z * chips + (my_y - bin_y) % chips) * CORES + (bin_core + my_core) % CORES
    got, base, pull, heads, gain, pieces, source, back_lane, count = lax.optimization_barrier(
        (got, base, pull, heads, gain, pieces, source, back_lane, count)
    )
    piece = samples * SEEN * quarter
    chosen_kv = call(
        select_kernel,
        on_chip((bands * samples * SEEN, quarter, 2 * channels), BF16),
        source,
        got,
        specs=[smem(), vmem()],
    )
    kv = lax.all_to_all(
        chosen_kv.reshape(bands, piece, 2 * channels), "mp", split_axis=0, concat_axis=0, tiled=True
    )
    bev_out, grads = call(
        attention_kernel,
        (
            jax.ShapeDtypeStruct((samples, queries, channels), BF16),
            on_chip((bands, piece, channels), BF16),
        ),
        count,
        kv,
        base,
        pull,
        heads,
        gain,
        specs=[smem(), vmem(), vmem(), pl.BlockSpec(memory_space=pltpu.HBM), vmem(), vmem()],
        scratch=[
            pltpu.VMEM((samples, queries, channels), F32),
            pltpu.SemaphoreType.DMA,
            pltpu.VMEM((bands, piece, HEADS * queries), F32),
            pltpu.VMEM((samples, bands * SEEN * quarter, HEADS * queries), BF16),
            pltpu.VMEM((samples, queries, channels), F32),
            pltpu.VMEM((samples, queries, channels), BF16),
        ],
    )
    grads, pieces = lax.optimization_barrier((grads, pieces))
    grads = lax.all_to_all(grads, "mp", split_axis=0, concat_axis=0, tiled=True)
    tokens = owners * quarter
    turned = call(
        functools.partial(turn_kernel, bands=bands, share=share),
        on_chip((depth, tokens), BF16),
        *pieces,
        specs=[pl.BlockSpec(memory_space=pltpu.HBM)] * len(pieces),
        scratch=[
            pltpu.VMEM((deep, len(pieces), quarter, depth), BF16),
            pltpu.VMEM((tokens // 128, depth, 128), F32),
            pltpu.SemaphoreType.DMA((len(pieces),)),
        ],
        cost=cost,
    )
    grads, turned = lax.optimization_barrier((grads, turned))
    back = call(
        return_kernel,
        on_chip((owners, quarter, channels), BF16),
        back_lane,
        grads.reshape(bands * samples * SEEN, quarter, channels),
        specs=[smem(), vmem()],
        scratch=[pltpu.VMEM((owners, quarter, channels), F32)],
    )

    def exchange(part, axis, groups):
        return lax.all_to_all(
            part, axis, split_axis=0, concat_axis=0, tiled=True, axis_index_groups=groups
        )

    columns = [[device(y, z, c) for z in zs] for y in ys for c in cs]
    back = exchange(back.reshape(deep, tokens // deep, channels), "dp", columns)
    neck = call(
        functools.partial(neck_kernel, samples=cams.shape[0]),
        on_chip((depth, channels), BF16),
        back.reshape(tokens, channels),
        turned,
    )
    planes = [
        [device(y, z, c) * bands + x for y in ys for c in cs for x in range(bands)] for z in zs
    ]
    neck = neck.reshape(chips * CORES * bands, share * deep, channels)
    neck = exchange(neck, ("dp", "mp"), planes).astype(F32)
    neck = jnp.sum(neck, axis=0).reshape(share, deep, channels).transpose(1, 0, 2)
    neck = exchange(neck, "dp", columns)
    return bev_out, jnp.sum(neck, axis=0)


def solution(mesh):
    return jax.shard_map(
        on_device,
        mesh=mesh,
        in_specs=(
            P(),
            P(),
            P("dp", None, None),
            P("dp", None, "mp"),
            P("dp", "mp", None),
            P("dp", "mp", None),
            P(),
            P("mp", None),
            P("dp", "mp", None),
            P(),
            P(),
            P("dp", "mp", None),
        ),
        out_specs=(P("dp", "mp", None), P(("dp", "mp"), None)),
        check_vma=False,
    )
```

```python
import functools

import jax
import jax.numpy as jnp
from jax import lax
from jax.experimental import pallas as pl
from jax.experimental.pallas import tpu as pltpu
from jax.sharding import PartitionSpec as P

HEADS = 8
KT = 4
CORES = 2
Y_CHIPS = 4
SEEN = 3

NORM_EPS = 1e-05
MASKED = -1e30
LOG2_E = 1.4426950408889634
BF16 = jnp.bfloat16
F32 = jnp.float32
I32 = jnp.int32


def dot(a, b, a_dim=1, b_dim=0):
    return lax.dot_general(a, b, (((a_dim,), (b_dim,)), ((), ())), preferred_element_type=F32)


def iota(shape, dim):
    return lax.broadcasted_iota(I32, shape, dim)


def vmem():
    return pl.BlockSpec(memory_space=pltpu.VMEM)


def smem():
    return pl.BlockSpec(memory_space=pltpu.SMEM)


def on_chip(shape, dtype):
    return pltpu.VMEM(shape, dtype)


def call(
    body, outs, *args, specs=None, out_specs=None, scratch=(), cost=(1 << 20, 1 << 20), pinned=True
):
    specs = specs or [vmem()] * len(args)
    if pinned:
        args = [
            pltpu.with_memory_space_constraint(arg, spec.memory_space) for arg, spec in zip(args, specs)
        ]
    return pl.pallas_call(
        body,
        out_shape=outs,
        in_specs=specs,
        out_specs=out_specs or jax.tree.map(lambda _: vmem(), outs),
        scratch_shapes=scratch,
        compiler_params=pltpu.CompilerParams(vmem_limit_bytes=24 << 20),
        cost_estimate=pl.CostEstimate(flops=cost[0], bytes_accessed=cost[1], transcendentals=0),
    )(*args)


def pack_kernel(
    bin_ref,
    cams_hbm,
    pack_hbm,
    image_hbm,
    key_hbm,
    weight_hbm,
    lane_ref,
    owner_ref,
    cams_ref,
    pack_ref,
    image_ref,
    key_ref,
    weight_ref,
    feature_ref,
    index_ref,
    sems,
    *,
    pack_slots,
):
    moves = [
        pltpu.make_async_copy(source, target, sems.at[i])
        for i, (source, target) in enumerate(
            (
                (cams_hbm, cams_ref),
                (pack_hbm, pack_ref),
                (image_hbm, image_ref),
                (weight_hbm, weight_ref),
                (key_hbm, key_ref),
            )
        )
    ]
    for move in moves:
        move.start()
    cameras = pack_ref.shape[1]
    rows, channels = key_ref.shape
    slots = pack_slots
    owners, quarter, _ = lane_ref.shape
    groups, width = cams_ref.shape
    spd = groups * width // owners
    moves[0].wait()
    first = iota((owners, width), 0) * spd
    before = jnp.zeros((owners, width), F32)
    for g in range(groups):
        counts = cams_ref[g : g + 1, :].astype(F32)
        before += jnp.where(iota((owners, width), 1) + g * width < first, counts, 0.0)
    start = jnp.sum(before, axis=1, keepdims=True)
    start = jnp.sum(
        jnp.where(iota((owners, owners), 0) == iota((owners, owners), 1), start, 0.0), axis=0, keepdims=True
    )
    moves[1].wait()
    here = (pack_ref[...] - bin_ref[0] * slots) == iota((slots, cameras), 0)
    number = iota((1, cameras), 1).astype(F32)
    camera = jnp.sum(jnp.where(here, number, 0.0), axis=1, keepdims=True)
    owner = jnp.sum((start <= camera).astype(F32), axis=1, keepdims=True) - 1.0
    across = (slots, owner_ref.shape[1])
    owner = jnp.sum(jnp.where(iota(across, 0) == iota(across, 1), owner, 0.0), axis=0, keepdims=True)
    owner_ref[...] = jnp.broadcast_to(owner, owner_ref.shape).astype(I32)
    index = pltpu.make_async_copy(owner_ref, index_ref, sems.at[5])
    index.start()
    moves[2].wait()
    moves[3].wait()
    feature_ref[...] = dot(image_ref[...], weight_ref[...]).astype(BF16)
    index.wait()
    moves[4].wait()
    for s in range(slots):
        here = slice(s * quarter, (s + 1) * quarter)
        lane_ref[index_ref[0, s], :, :channels] = feature_ref[here, :]
        lane_ref[index_ref[0, s], :, channels:] = key_ref[here, :]


def deal_kernel(lane_ref, image_ref, out_ref):
    quarter = out_ref.shape[1]
    out_ref[...] = jnp.zeros(out_ref.shape, BF16)
    for s in range(image_ref.shape[0] // quarter):
        out_ref[lane_ref[s]] = image_ref[s * quarter : (s + 1) * quarter, :]


def turn_kernel(*refs, bands, share):
    out_ref, block_ref, turned_ref, sems = refs[-4:]
    pieces = refs[:-4]
    deep, quarter, _ = pieces[0].shape
    moves = [
        pltpu.make_async_copy(piece, block_ref.at[:, p], sems.at[p]) for p, piece in enumerate(pieces)
    ]
    for move in moves:
        move.start()
    for move in moves:
        move.wait()
    groups, depth, width = turned_ref.shape
    some = width // (len(pieces) * quarter)
    for g in range(groups):
        block = block_ref[g * some : (g + 1) * some].reshape(width, depth)
        turned_ref[g] = block.astype(F32).T
    step = CORES * bands * share
    at = 0
    for y in range(len(pieces) // CORES):
        for c in range(CORES):
            for j in range(bands * share):
                first = y * deep * step + c * bands * share + j
                for g in range(groups):
                    part = turned_ref.at[g][pl.ds(first, deep, stride=step), :]
                    out_ref[at : at + deep, g * width : (g + 1) * width] = part.astype(BF16)
                at += deep


def temporal_kernel(
    band_ref,
    query_ref,
    point_ref,
    prev_ref,
    align_ref,
    cotangent_ref,
    gain_ref,
    base_ref,
    pull_ref,
    heads_ref,
    scale_ref,
):
    samples, cells, channels = prev_ref.shape
    query = query_ref[...]
    head_dim = channels // HEADS
    wide = query.astype(F32)
    gain = gain_ref[...]
    scale_ref[...] = gain
    for h in range(HEADS):
        mask = (iota((1, channels), 1) // head_dim == h).astype(F32).astype(BF16)
        heads_ref[h * cells : (h + 1) * cells, :] = query * mask
    gates = []
    for k in range(KT):
        shape = (HEADS * KT, channels)
        pick = iota(shape, 0) == (iota(shape, 1) // head_dim) * KT + k
        weight = dot(point_ref[...], pick.astype(F32).astype(BF16)).astype(BF16)
        gates.append(jax.nn.sigmoid(dot(query, weight)))
    for m in range(samples):
        total = wide
        for k in range(KT):
            cell = align_ref[m, k : k + 1, :] - band_ref[0] * cells
            pick = (iota((cells, cells), 0) == cell).astype(F32).astype(BF16)
            total = total + gates[k] * dot(pick, prev_ref[m], 0, 0)
        base_ref[m] = total
        pull = cotangent_ref[m].astype(F32) * gain
        pull_ref[m] = pull - jnp.mean(pull, axis=1, keepdims=True)


def select_kernel(source_ref, lane_ref, out_ref):
    for e in range(out_ref.shape[0]):
        out_ref[e] = lane_ref[source_ref[e]]


def attention_kernel(
    count_ref,
    kv_ref,
    base_ref,
    pull_hbm,
    heads_ref,
    gain_ref,
    out_hbm,
    grad_ref,
    out_ref,
    pull_ref,
    sem,
    out_sems,
    score_ref,
    prob_ref,
    norm_ref,
    cross_ref,
):
    move = pltpu.make_async_copy(pull_hbm, pull_ref, sem)
    move.start()
    parts, rows, width = kv_ref.shape
    samples, queries, channels = base_ref.shape
    step = rows // samples
    keys = parts * step
    head_dim = channels // HEADS
    quarter = step // SEEN
    gain = gain_ref[...]
    lane_head = iota((1, channels), 1) // head_dim
    masks = [(lane_head == h).astype(F32).astype(BF16) for h in range(HEADS)]
    factor = float(head_dim) ** -0.5 * LOG2_E
    place = iota((keys, HEADS * queries), 0) % step // quarter
    spans = [slice(m * step, (m + 1) * step) for m in range(samples)]
    ray = kv_ref[:, :, channels:].reshape(parts * rows, channels)
    score_ref[...] = dot(ray, heads_ref[...], 1, 1).reshape(score_ref.shape)
    for m in range(samples):
        scores = score_ref[:, spans[m], :].reshape(keys, HEADS * queries)
        scores = jnp.where(place < count_ref[m], scores, MASKED)
        raised = jnp.exp2((scores - jnp.max(scores, axis=0, keepdims=True)) * factor)
        prob_ref[m] = (raised * (1.0 / jnp.sum(raised, axis=0, keepdims=True))).astype(BF16)
    for m in range(samples):
        values = kv_ref[:, spans[m], :channels].reshape(keys, channels)
        values = jnp.concatenate([values * mask for mask in masks], axis=0)
        probs = prob_ref[m]
        tall = jnp.concatenate(
            [probs[:, h * queries : (h + 1) * queries] for h in range(HEADS)], axis=0
        )
        norm_ref[m] = base_ref[m] + dot(tall, values, 0, 0)
    move.wait()
    written = []
    for m in range(samples):
        pre_norm = norm_ref[m]
        centred = pre_norm - jnp.mean(pre_norm, axis=1, keepdims=True)
        scale = lax.rsqrt(jnp.mean(centred * centred, axis=1, keepdims=True) + NORM_EPS)
        unit = centred * scale
        out_ref[m] = (unit * gain).astype(BF16)
        written.append(pltpu.make_async_copy(out_ref.at[m], out_hbm.at[m], out_sems.at[m]))
        written[m].start()
        pull = pull_ref[m]
        pull = pull - unit * jnp.mean(pull * unit, axis=1, keepdims=True)
        cross_ref[m] = (pull * scale).astype(BF16)
    for m in range(samples):
        pull = cross_ref[m]
        pull = jnp.concatenate([pull * mask for mask in masks], axis=0)
        grad_ref[:, spans[m], :] = dot(prob_ref[m], pull).astype(BF16).reshape(parts, step, channels)
    for move in written:
        move.wait()


def return_kernel(source_ref, grad_ref, lane_ref, sum_ref):
    sum_ref[...] = jnp.zeros(sum_ref.shape, F32)
    for e in range(grad_ref.shape[0]):
        lane = source_ref[e]
        sum_ref[lane] = sum_ref[lane] + grad_ref[e].astype(F32)
    lane_ref[...] = sum_ref[...].astype(BF16)


def neck_kernel(grad_ref, turned_ref, out_ref, *, samples):
    out_ref[...] = (dot(turned_ref[...], grad_ref[...]) * (1.0 / samples)).astype(BF16)


def on_device(
    cams,
    pack,
    visible,
    align,
    images,
    cam_keys,
    neck_weight,
    bev_query,
    prev_bev,
    point_weight,
    norm_gain,
    out_grad,
):
    owners = lax.axis_size("dp")
    bands = lax.axis_size("mp")
    owner_id = lax.axis_index("dp").astype(I32)
    band_id = lax.axis_index("mp").astype(I32)
    samples, max_cams, _ = visible.shape
    slots, quarter, depth = images.shape
    channels = neck_weight.shape[1]
    queries = bev_query.shape[0]
    rows = slots * quarter
    flat_images = images.reshape(rows, depth)
    lanes, owner = call(
        functools.partial(pack_kernel, pack_slots=slots),
        (
            jax.ShapeDtypeStruct((owners, quarter, 2 * channels), BF16),
            jax.ShapeDtypeStruct((8, 128), I32),
        ),
        owner_id[None],
        *(
            pltpu.with_memory_space_constraint(arg, pltpu.HBM)
            for arg in (
                cams.reshape(-1, min(128, cams.shape[0])),
                pack[None],
                flat_images,
                cam_keys.reshape(rows, channels),
                neck_weight,
            )
        ),
        specs=[smem()] + [pl.BlockSpec(memory_space=pltpu.HBM)] * 5,
        scratch=[
            pltpu.VMEM((cams.shape[0] // min(128, cams.shape[0]), min(128, cams.shape[0])), I32),
            pltpu.VMEM((1, pack.shape[0]), I32),
            pltpu.VMEM((rows, depth), BF16),
            pltpu.VMEM((rows, channels), BF16),
            pltpu.VMEM((depth, channels), BF16),
            pltpu.VMEM((rows, channels), BF16),
            pltpu.SMEM((8, 128), I32),
            pltpu.SemaphoreType.DMA((6,)),
        ],
        pinned=False,
    )
    got = lax.all_to_all(lanes, "dp", split_axis=0, concat_axis=0, tiled=True)
    cost = 1 << 30, 1 << 22
    chips = Y_CHIPS
    deep = owners // (CORES * chips)
    share = depth // (owners * bands)

    def device(y, z, c):
        return (y * deep + z) * CORES + c

    def place_of(device_id):
        return device_id // (deep * CORES), device_id // CORES % deep, device_id % CORES

    ys, zs, cs = range(chips), range(deep), range(CORES)
    my_y, _, my_core = place_of(owner_id)
    owner_y, owner_z, owner_core = place_of(owner[0, :slots])
    column = (owner_y - my_y) % chips * CORES + (owner_core + my_core) % CORES
    dealt = call(
        deal_kernel,
        jax.ShapeDtypeStruct((owners, quarter, depth), BF16),
        column * deep + owner_z,
        flat_images,
        specs=[smem(), vmem()],
        cost=cost,
    ).reshape(chips * CORES, deep, quarter, depth)
    pieces = [dealt[0]]
    for p in range(1, chips * CORES):
        moves = [
            (device(y, z, c), device((y + p // CORES) % chips, z, (c + p) % CORES))
            for y in ys
            for z in zs
            for c in cs
        ]
        pieces.append(lax.ppermute(dealt[p], "dp", moves))
    base, pull, heads, gain = call(
        temporal_kernel,
        (
            on_chip((samples, queries, channels), F32),
            pltpu.HBM((samples, queries, channels), F32),
            on_chip((HEADS * queries, channels), BF16),
            on_chip((1, channels), F32),
        ),
        band_id[None],
        bev_query,
        point_weight,
        prev_bev,
        align,
        out_grad,
        norm_gain[None],
        specs=[smem()] + [vmem()] * 6,
        cost=cost,
    )
    first = owner_id * samples
    sample_ids = jnp.arange(cams.shape[0], dtype=I32)
    start = jnp.sum(jnp.where(sample_ids < first, cams, 0))
    local = lax.dynamic_slice(cams, (first,), (samples,))
    window = samples * max_cams
    padded = jnp.concatenate([pack, jnp.zeros((window,), I32)])
    bins = lax.dynamic_slice(padded, (start,), (window,)) // slots
    member = jnp.arange(samples, dtype=I32)
    offset = jnp.sum(jnp.where(member[None, :] < member[:, None], local[None, :], 0), axis=1)
    camera = jnp.arange(max_cams, dtype=I32)
    seen = (visible > 0).astype(I32)
    earlier = (camera[:, None] < camera[None, :]).astype(I32)
    rank = jnp.sum(seen[:, :, None, :] * earlier[None, :, :, None], axis=1)
    place = jnp.arange(SEEN, dtype=I32)
    chosen = (rank[:, :, :, None] == place) & (seen[:, :, :, None] > 0)
    position = jnp.sum(
        jnp.where(chosen, offset[:, None, None, None] + camera[None, :, None, None] + 1, 0), axis=1
    )
    in_window = position[..., None] == jnp.arange(1, window + 1, dtype=I32)
    lane_of = jnp.sum(jnp.where(in_window, bins + 1, 0), axis=-1) - 1
    lane_of = jnp.where(lane_of >= 0, lane_of, lane_of[:, :, :1])
    lane_of = lane_of.transpose(1, 0, 2).reshape(bands * samples * SEEN)
    count = lax.dynamic_slice_in_dim(jnp.sum(seen, axis=1), band_id, 1, axis=1)[:, 0]
    source = jnp.maximum(lane_of, 0)
    bin_y, bin_z, bin_core = place_of(source)
    back_lane = (bin_z * chips + (my_y - bin_y) % chips) * CORES + (bin_core + my_core) % CORES
    got, base, pull, heads, gain, pieces, source, back_lane, count = lax.optimization_barrier(
        (got, base, pull, heads, gain, pieces, source, back_lane, count)
    )
    piece = samples * SEEN * quarter
    chosen_kv = call(
        select_kernel,
        on_chip((bands * samples * SEEN, quarter, 2 * channels), BF16),
        source,
        got,
        specs=[smem(), vmem()],
    )
    kv = lax.all_to_all(
        chosen_kv.reshape(bands, piece, 2 * channels), "mp", split_axis=0, concat_axis=0, tiled=True
    )
    bev_out, grads = call(
        attention_kernel,
        (
            jax.ShapeDtypeStruct((samples, queries, channels), BF16),
            on_chip((bands, piece, channels), BF16),
        ),
        count,
        kv,
        base,
        pull,
        heads,
        gain,
        specs=[smem(), vmem(), vmem(), pl.BlockSpec(memory_space=pltpu.HBM), vmem(), vmem()],
        out_specs=(pl.BlockSpec(memory_space=pltpu.HBM), vmem()),
        scratch=[
            pltpu.VMEM((samples, queries, channels), BF16),
            pltpu.VMEM((samples, queries, channels), F32),
            pltpu.SemaphoreType.DMA,
            pltpu.SemaphoreType.DMA((samples,)),
            pltpu.VMEM((bands, piece, HEADS * queries), F32),
            pltpu.VMEM((samples, bands * SEEN * quarter, HEADS * queries), BF16),
            pltpu.VMEM((samples, queries, channels), F32),
            pltpu.VMEM((samples, queries, channels), BF16),
        ],
    )
    grads = lax.all_to_all(grads, "mp", split_axis=0, concat_axis=0, tiled=True)
    grads, pieces = lax.optimization_barrier((grads, pieces))
    back = call(
        return_kernel,
        on_chip((owners, quarter, channels), BF16),
        back_lane,
        grads.reshape(bands * samples * SEEN, quarter, channels),
        specs=[smem(), vmem()],
        scratch=[pltpu.VMEM((owners, quarter, channels), F32)],
    )

    def exchange(part, axis, groups):
        return lax.all_to_all(
            part, axis, split_axis=0, concat_axis=0, tiled=True, axis_index_groups=groups
        )

    columns = [[device(y, z, c) for z in zs] for y in ys for c in cs]
    tokens = owners * quarter
    turned = call(
        functools.partial(turn_kernel, bands=bands, share=share),
        on_chip((depth, tokens), BF16),
        *pieces,
        specs=[pl.BlockSpec(memory_space=pltpu.HBM)] * len(pieces),
        scratch=[
            pltpu.VMEM((deep, len(pieces), quarter, depth), BF16),
            pltpu.VMEM((tokens // 128, depth, 128), F32),
            pltpu.SemaphoreType.DMA((len(pieces),)),
        ],
        cost=cost,
    )
    back = exchange(back.reshape(deep, tokens // deep, channels), "dp", columns)
    neck = call(
        functools.partial(neck_kernel, samples=cams.shape[0]),
        on_chip((depth, channels), BF16),
        back.reshape(tokens, channels),
        turned,
    )
    planes = [
        [device(y, z, c) * bands + x for y in ys for c in cs for x in range(bands)] for z in zs
    ]
    neck = neck.reshape(chips * CORES * bands, share * deep, channels)
    neck = exchange(neck, ("dp", "mp"), planes).astype(F32)
    neck = jnp.sum(neck, axis=0).reshape(share, deep, channels).transpose(1, 0, 2)
    neck = exchange(neck, "dp", columns)
    return bev_out, jnp.sum(neck, axis=0)


def solution(mesh):
    return jax.shard_map(
        on_device,
        mesh=mesh,
        in_specs=(
            P(),
            P(),
            P("dp", None, None),
            P("dp", None, "mp"),
            P("dp", "mp", None),
            P("dp", "mp", None),
            P(),
            P("mp", None),
            P("dp", "mp", None),
            P(),
            P(),
            P("dp", "mp", None),
        ),
        out_specs=(P("dp", "mp", None), P(("dp", "mp"), None)),
        check_vma=False,
    )
```

```python
import functools

import jax
import jax.numpy as jnp
from jax import lax
from jax.experimental import pallas as pl
from jax.experimental.pallas import tpu as pltpu
from jax.sharding import PartitionSpec as P

HEADS = 8
KT = 4
CORES = 2
Y_CHIPS = 4
SEEN = 3

NORM_EPS = 1e-05
MASKED = -1e30
LOG2_E = 1.4426950408889634
BF16 = jnp.bfloat16
F32 = jnp.float32
I32 = jnp.int32


def dot(a, b, a_dim=1, b_dim=0):
    return lax.dot_general(a, b, (((a_dim,), (b_dim,)), ((), ())), preferred_element_type=F32)


def iota(shape, dim):
    return lax.broadcasted_iota(I32, shape, dim)


def vmem():
    return pl.BlockSpec(memory_space=pltpu.VMEM)


def smem():
    return pl.BlockSpec(memory_space=pltpu.SMEM)


def on_chip(shape, dtype):
    return pltpu.VMEM(shape, dtype)


def call(
    body, outs, *args, specs=None, out_specs=None, scratch=(), cost=(1 << 20, 1 << 20), pinned=True
):
    specs = specs or [vmem()] * len(args)
    if pinned:
        args = [
            pltpu.with_memory_space_constraint(arg, spec.memory_space) for arg, spec in zip(args, specs)
        ]
    return pl.pallas_call(
        body,
        out_shape=outs,
        in_specs=specs,
        out_specs=out_specs or jax.tree.map(lambda _: vmem(), outs),
        scratch_shapes=scratch,
        compiler_params=pltpu.CompilerParams(vmem_limit_bytes=24 << 20),
        cost_estimate=pl.CostEstimate(flops=cost[0], bytes_accessed=cost[1], transcendentals=0),
    )(*args)


def pack_kernel(
    bin_ref,
    cams_hbm,
    pack_hbm,
    image_hbm,
    key_hbm,
    weight_hbm,
    lane_ref,
    owner_ref,
    cams_ref,
    pack_ref,
    image_ref,
    key_ref,
    weight_ref,
    feature_ref,
    index_ref,
    sems,
    *,
    pack_slots,
):
    moves = [
        pltpu.make_async_copy(source, target, sems.at[i])
        for i, (source, target) in enumerate(
            (
                (cams_hbm, cams_ref),
                (pack_hbm, pack_ref),
                (image_hbm, image_ref),
                (weight_hbm, weight_ref),
                (key_hbm, key_ref),
            )
        )
    ]
    for move in moves:
        move.start()
    cameras = pack_ref.shape[1]
    rows, channels = key_ref.shape
    slots = pack_slots
    owners, quarter, _ = lane_ref.shape
    groups, width = cams_ref.shape
    spd = groups * width // owners
    moves[0].wait()
    first = iota((owners, width), 0) * spd
    before = jnp.zeros((owners, width), F32)
    for g in range(groups):
        counts = cams_ref[g : g + 1, :].astype(F32)
        before += jnp.where(iota((owners, width), 1) + g * width < first, counts, 0.0)
    start = jnp.sum(before, axis=1, keepdims=True)
    start = jnp.sum(
        jnp.where(iota((owners, owners), 0) == iota((owners, owners), 1), start, 0.0), axis=0, keepdims=True
    )
    moves[1].wait()
    here = (pack_ref[...] - bin_ref[0] * slots) == iota((slots, cameras), 0)
    number = iota((1, cameras), 1).astype(F32)
    camera = jnp.sum(jnp.where(here, number, 0.0), axis=1, keepdims=True)
    owner = jnp.sum((start <= camera).astype(F32), axis=1, keepdims=True) - 1.0
    across = (slots, owner_ref.shape[1])
    owner = jnp.sum(jnp.where(iota(across, 0) == iota(across, 1), owner, 0.0), axis=0, keepdims=True)
    owner_ref[...] = jnp.broadcast_to(owner, owner_ref.shape).astype(I32)
    index = pltpu.make_async_copy(owner_ref, index_ref, sems.at[5])
    index.start()
    moves[2].wait()
    moves[3].wait()
    feature_ref[...] = dot(image_ref[...], weight_ref[...]).astype(BF16)
    index.wait()
    moves[4].wait()
    for s in range(slots):
        here = slice(s * quarter, (s + 1) * quarter)
        lane_ref[index_ref[0, s], :, :channels] = feature_ref[here, :]
        lane_ref[index_ref[0, s], :, channels:] = key_ref[here, :]


def deal_kernel(lane_ref, image_ref, out_ref):
    quarter = out_ref.shape[1]
    out_ref[...] = jnp.zeros(out_ref.shape, BF16)
    for s in range(image_ref.shape[0] // quarter):
        out_ref[lane_ref[s]] = image_ref[s * quarter : (s + 1) * quarter, :]


def turn_kernel(*refs, bands, share):
    out_ref, block_ref, turned_ref, sems = refs[-4:]
    pieces = refs[:-4]
    deep, quarter, _ = pieces[0].shape
    moves = [
        pltpu.make_async_copy(piece, block_ref.at[:, p], sems.at[p]) for p, piece in enumerate(pieces)
    ]
    for move in moves:
        move.start()
    for move in moves:
        move.wait()
    groups, depth, width = turned_ref.shape
    some = width // (len(pieces) * quarter)
    for g in range(groups):
        block = block_ref[g * some : (g + 1) * some].reshape(width, depth)
        turned_ref[g] = block.astype(F32).T
    step = CORES * bands * share
    at = 0
    for y in range(len(pieces) // CORES):
        for band in range(bands):
            for c in range(CORES):
                for i in range(share):
                    first = y * deep * step + (c * bands + band) * share + i
                    for g in range(groups):
                        part = turned_ref.at[g][pl.ds(first, deep, stride=step), :]
                        out_ref[at : at + deep, g * width : (g + 1) * width] = part.astype(BF16)
                    at += deep


def temporal_kernel(
    band_ref,
    query_ref,
    point_ref,
    prev_ref,
    align_ref,
    cotangent_ref,
    gain_ref,
    base_ref,
    pull_ref,
    heads_ref,
    scale_ref,
):
    samples, cells, channels = prev_ref.shape
    query = query_ref[...]
    head_dim = channels // HEADS
    wide = query.astype(F32)
    gain = gain_ref[...]
    scale_ref[...] = gain
    for h in range(HEADS):
        mask = (iota((1, channels), 1) // head_dim == h).astype(F32).astype(BF16)
        heads_ref[h * cells : (h + 1) * cells, :] = query * mask
    gates = []
    for k in range(KT):
        shape = (HEADS * KT, channels)
        pick = iota(shape, 0) == (iota(shape, 1) // head_dim) * KT + k
        weight = dot(point_ref[...], pick.astype(F32).astype(BF16)).astype(BF16)
        gates.append(jax.nn.sigmoid(dot(query, weight)))
    for m in range(samples):
        total = wide
        for k in range(KT):
            cell = align_ref[m, k : k + 1, :] - band_ref[0] * cells
            pick = (iota((cells, cells), 0) == cell).astype(F32).astype(BF16)
            total = total + gates[k] * dot(pick, prev_ref[m], 0, 0)
        base_ref[m] = total
        pull = cotangent_ref[m].astype(F32) * gain
        pull_ref[m] = pull - jnp.mean(pull, axis=1, keepdims=True)


def select_kernel(source_ref, lane_ref, out_ref):
    for e in range(out_ref.shape[0]):
        out_ref[e] = lane_ref[source_ref[e]]


def attention_kernel(
    count_ref,
    kv_ref,
    base_ref,
    pull_hbm,
    heads_ref,
    gain_ref,
    out_hbm,
    grad_ref,
    out_ref,
    pull_ref,
    sem,
    out_sems,
    score_ref,
    prob_ref,
    norm_ref,
    cross_ref,
):
    move = pltpu.make_async_copy(pull_hbm, pull_ref, sem)
    move.start()
    parts, rows, width = kv_ref.shape
    samples, queries, channels = base_ref.shape
    step = rows // samples
    keys = parts * step
    head_dim = channels // HEADS
    quarter = step // SEEN
    gain = gain_ref[...]
    lane_head = iota((1, channels), 1) // head_dim
    masks = [(lane_head == h).astype(F32).astype(BF16) for h in range(HEADS)]
    factor = float(head_dim) ** -0.5 * LOG2_E
    place = iota((keys, HEADS * queries), 0) % step // quarter
    spans = [slice(m * step, (m + 1) * step) for m in range(samples)]
    ray = kv_ref[:, :, channels:].reshape(parts * rows, channels)
    score_ref[...] = dot(ray, heads_ref[...], 1, 1).reshape(score_ref.shape)
    for m in range(samples):
        scores = score_ref[:, spans[m], :].reshape(keys, HEADS * queries)
        scores = jnp.where(place < count_ref[m], scores, MASKED)
        raised = jnp.exp2((scores - jnp.max(scores, axis=0, keepdims=True)) * factor)
        prob_ref[m] = (raised * (1.0 / jnp.sum(raised, axis=0, keepdims=True))).astype(BF16)
    for m in range(samples):
        values = kv_ref[:, spans[m], :channels].reshape(keys, channels)
        values = jnp.concatenate([values * mask for mask in masks], axis=0)
        probs = prob_ref[m]
        tall = jnp.concatenate(
            [probs[:, h * queries : (h + 1) * queries] for h in range(HEADS)], axis=0
        )
        norm_ref[m] = base_ref[m] + dot(tall, values, 0, 0)
    move.wait()
    written = []
    for m in range(samples):
        pre_norm = norm_ref[m]
        centred = pre_norm - jnp.mean(pre_norm, axis=1, keepdims=True)
        scale = lax.rsqrt(jnp.mean(centred * centred, axis=1, keepdims=True) + NORM_EPS)
        unit = centred * scale
        out_ref[m] = (unit * gain).astype(BF16)
        written.append(pltpu.make_async_copy(out_ref.at[m], out_hbm.at[m], out_sems.at[m]))
        written[m].start()
        pull = pull_ref[m]
        pull = pull - unit * jnp.mean(pull * unit, axis=1, keepdims=True)
        cross_ref[m] = (pull * scale).astype(BF16)
    for m in range(samples):
        pull = cross_ref[m]
        pull = jnp.concatenate([pull * mask for mask in masks], axis=0)
        grad_ref[:, spans[m], :] = dot(prob_ref[m], pull).astype(BF16).reshape(parts, step, channels)
    for move in written:
        move.wait()


def return_kernel(source_ref, grad_ref, lane_ref, sum_ref):
    sum_ref[...] = jnp.zeros(sum_ref.shape, F32)
    for e in range(grad_ref.shape[0]):
        lane = source_ref[e]
        sum_ref[lane] = sum_ref[lane] + grad_ref[e].astype(F32)
    lane_ref[...] = sum_ref[...].astype(BF16)


def neck_kernel(grad_ref, turned_ref, out_ref, *, samples):
    out_ref[...] = (dot(turned_ref[...], grad_ref[...]) * (1.0 / samples)).astype(BF16)


def on_device(
    cams,
    pack,
    visible,
    align,
    images,
    cam_keys,
    neck_weight,
    bev_query,
    prev_bev,
    point_weight,
    norm_gain,
    out_grad,
):
    owners = lax.axis_size("dp")
    bands = lax.axis_size("mp")
    owner_id = lax.axis_index("dp").astype(I32)
    band_id = lax.axis_index("mp").astype(I32)
    samples, max_cams, _ = visible.shape
    slots, quarter, depth = images.shape
    channels = neck_weight.shape[1]
    queries = bev_query.shape[0]
    rows = slots * quarter
    flat_images = images.reshape(rows, depth)
    lanes, owner = call(
        functools.partial(pack_kernel, pack_slots=slots),
        (
            jax.ShapeDtypeStruct((owners, quarter, 2 * channels), BF16),
            jax.ShapeDtypeStruct((8, 128), I32),
        ),
        owner_id[None],
        *(
            pltpu.with_memory_space_constraint(arg, pltpu.HBM)
            for arg in (
                cams.reshape(-1, min(128, cams.shape[0])),
                pack[None],
                flat_images,
                cam_keys.reshape(rows, channels),
                neck_weight,
            )
        ),
        specs=[smem()] + [pl.BlockSpec(memory_space=pltpu.HBM)] * 5,
        scratch=[
            pltpu.VMEM((cams.shape[0] // min(128, cams.shape[0]), min(128, cams.shape[0])), I32),
            pltpu.VMEM((1, pack.shape[0]), I32),
            pltpu.VMEM((rows, depth), BF16),
            pltpu.VMEM((rows, channels), BF16),
            pltpu.VMEM((depth, channels), BF16),
            pltpu.VMEM((rows, channels), BF16),
            pltpu.SMEM((8, 128), I32),
            pltpu.SemaphoreType.DMA((6,)),
        ],
        pinned=False,
    )
    got = lax.all_to_all(lanes, "dp", split_axis=0, concat_axis=0, tiled=True)
    cost = 1 << 30, 1 << 22
    chips = Y_CHIPS
    deep = owners // (CORES * chips)
    share = depth // (owners * bands)

    def device(y, z, c):
        return (y * deep + z) * CORES + c

    def place_of(device_id):
        return device_id // (deep * CORES), device_id // CORES % deep, device_id % CORES

    ys, zs, cs = range(chips), range(deep), range(CORES)
    my_y, _, my_core = place_of(owner_id)
    owner_y, owner_z, owner_core = place_of(owner[0, :slots])
    column = (owner_y - my_y) % chips * CORES + (owner_core + my_core) % CORES
    dealt = call(
        deal_kernel,
        jax.ShapeDtypeStruct((owners, quarter, depth), BF16),
        column * deep + owner_z,
        flat_images,
        specs=[smem(), vmem()],
        cost=cost,
    ).reshape(chips * CORES, deep, quarter, depth)
    pieces = [dealt[0]]
    for p in range(1, chips * CORES):
        moves = [
            (device(y, z, c), device((y + p // CORES) % chips, z, (c + p) % CORES))
            for y in ys
            for z in zs
            for c in cs
        ]
        pieces.append(lax.ppermute(dealt[p], "dp", moves))
    base, pull, heads, gain = call(
        temporal_kernel,
        (
            on_chip((samples, queries, channels), F32),
            pltpu.HBM((samples, queries, channels), F32),
            on_chip((HEADS * queries, channels), BF16),
            on_chip((1, channels), F32),
        ),
        band_id[None],
        bev_query,
        point_weight,
        prev_bev,
        align,
        out_grad,
        norm_gain[None],
        specs=[smem()] + [vmem()] * 6,
        cost=cost,
    )
    first = owner_id * samples
    sample_ids = jnp.arange(cams.shape[0], dtype=I32)
    start = jnp.sum(jnp.where(sample_ids < first, cams, 0))
    local = lax.dynamic_slice(cams, (first,), (samples,))
    window = samples * max_cams
    padded = jnp.concatenate([pack, jnp.zeros((window,), I32)])
    bins = lax.dynamic_slice(padded, (start,), (window,)) // slots
    member = jnp.arange(samples, dtype=I32)
    offset = jnp.sum(jnp.where(member[None, :] < member[:, None], local[None, :], 0), axis=1)
    camera = jnp.arange(max_cams, dtype=I32)
    seen = (visible > 0).astype(I32)
    earlier = (camera[:, None] < camera[None, :]).astype(I32)
    rank = jnp.sum(seen[:, :, None, :] * earlier[None, :, :, None], axis=1)
    place = jnp.arange(SEEN, dtype=I32)
    chosen = (rank[:, :, :, None] == place) & (seen[:, :, :, None] > 0)
    position = jnp.sum(
        jnp.where(chosen, offset[:, None, None, None] + camera[None, :, None, None] + 1, 0), axis=1
    )
    in_window = position[..., None] == jnp.arange(1, window + 1, dtype=I32)
    lane_of = jnp.sum(jnp.where(in_window, bins + 1, 0), axis=-1) - 1
    lane_of = jnp.where(lane_of >= 0, lane_of, lane_of[:, :, :1])
    lane_of = lane_of.transpose(1, 0, 2).reshape(bands * samples * SEEN)
    count = lax.dynamic_slice_in_dim(jnp.sum(seen, axis=1), band_id, 1, axis=1)[:, 0]
    source = jnp.maximum(lane_of, 0)
    bin_y, bin_z, bin_core = place_of(source)
    back_lane = (bin_z * chips + (my_y - bin_y) % chips) * CORES + (bin_core + my_core) % CORES
    got, base, pull, heads, gain, pieces, source, back_lane, count = lax.optimization_barrier(
        (got, base, pull, heads, gain, pieces, source, back_lane, count)
    )
    piece = samples * SEEN * quarter
    chosen_kv = call(
        select_kernel,
        on_chip((bands * samples * SEEN, quarter, 2 * channels), BF16),
        source,
        got,
        specs=[smem(), vmem()],
    )
    kv = lax.all_to_all(
        chosen_kv.reshape(bands, piece, 2 * channels), "mp", split_axis=0, concat_axis=0, tiled=True
    )
    bev_out, grads = call(
        attention_kernel,
        (
            jax.ShapeDtypeStruct((samples, queries, channels), BF16),
            on_chip((bands, piece, channels), BF16),
        ),
        count,
        kv,
        base,
        pull,
        heads,
        gain,
        specs=[smem(), vmem(), vmem(), pl.BlockSpec(memory_space=pltpu.HBM), vmem(), vmem()],
        out_specs=(pl.BlockSpec(memory_space=pltpu.HBM), vmem()),
        scratch=[
            pltpu.VMEM((samples, queries, channels), BF16),
            pltpu.VMEM((samples, queries, channels), F32),
            pltpu.SemaphoreType.DMA,
            pltpu.SemaphoreType.DMA((samples,)),
            pltpu.VMEM((bands, piece, HEADS * queries), F32),
            pltpu.VMEM((samples, bands * SEEN * quarter, HEADS * queries), BF16),
            pltpu.VMEM((samples, queries, channels), F32),
            pltpu.VMEM((samples, queries, channels), BF16),
        ],
    )
    grads = lax.all_to_all(grads, "mp", split_axis=0, concat_axis=0, tiled=True)
    grads, pieces = lax.optimization_barrier((grads, pieces))
    back = call(
        return_kernel,
        on_chip((owners, quarter, channels), BF16),
        back_lane,
        grads.reshape(bands * samples * SEEN, quarter, channels),
        specs=[smem(), vmem()],
        scratch=[pltpu.VMEM((owners, quarter, channels), F32)],
    )

    def exchange(part, axis, groups):
        return lax.all_to_all(
            part, axis, split_axis=0, concat_axis=0, tiled=True, axis_index_groups=groups
        )

    columns = [[device(y, z, c) for z in zs] for y in ys for c in cs]
    tokens = owners * quarter
    turned = call(
        functools.partial(turn_kernel, bands=bands, share=share),
        on_chip((depth, tokens), BF16),
        *pieces,
        specs=[pl.BlockSpec(memory_space=pltpu.HBM)] * len(pieces),
        scratch=[
            pltpu.VMEM((deep, len(pieces), quarter, depth), BF16),
            pltpu.VMEM((tokens // 128, depth, 128), F32),
            pltpu.SemaphoreType.DMA((len(pieces),)),
        ],
        cost=cost,
    )
    back = exchange(back.reshape(deep, tokens // deep, channels), "dp", columns)
    neck = call(
        functools.partial(neck_kernel, samples=cams.shape[0]),
        on_chip((depth, channels), BF16),
        back.reshape(tokens, channels),
        turned,
    )
    squares = [
        [device(y, z, c) * bands + x for y in ys for x in range(bands)] for z in zs for c in cs
    ]
    lines = [[device(y, z, c) for z in zs for c in cs] for y in ys]
    neck = neck.reshape(chips * bands, CORES * share * deep, channels)
    neck = exchange(neck, ("dp", "mp"), squares).astype(F32)
    neck = jnp.sum(neck, axis=0).reshape(CORES, share, deep, channels).transpose(2, 0, 1, 3)
    neck = exchange(neck.reshape(deep * CORES, share, channels), "dp", lines)
    return bev_out, jnp.sum(neck, axis=0)


def solution(mesh):
    return jax.shard_map(
        on_device,
        mesh=mesh,
        in_specs=(
            P(),
            P(),
            P("dp", None, None),
            P("dp", None, "mp"),
            P("dp", "mp", None),
            P("dp", "mp", None),
            P(),
            P("mp", None),
            P("dp", "mp", None),
            P(),
            P(),
            P("dp", "mp", None),
        ),
        out_specs=(P("dp", "mp", None), P(("dp", "mp"), None)),
        check_vma=False,
    )
```
